256 devices in a mesh: ctx: 32 (over x, y, core), head: 8 (over z).
Axes of the slice: x: 4, y: 4, z: 8, core: 2. Of those that a mesh axis runs over, the one named last changes fastest.
Arguments:
- queries: bfloat16 [4096, 128, 128], P('ctx', 'head'), may hold values from -64 to 64
- key_states: bfloat16 [4096, 8, 128], P('ctx', 'head'), may hold values from -4 to 4
- value_vector_states: bfloat16 [4096, 8, 128], P('ctx', 'head'), may hold values from -6 to 6
- map_query: float32 [128, 128, 64], P('head'), may hold values from -0.5 to 0.5
- map_key: float32 [128, 128, 64], P('head'), may hold values from -0.5 to 0.5
Outputs:
- grad_map_query: float32 [128, 128, 64], P('head')
- grad_map_key: float32 [128, 128, 64], P('head')
The draws below stay inside these ranges and needn't reach their ends.
All inputs are finite; a program needn't handle non-finite values.
Results may differ from the reference program's by a relative error of at most 0.0012.
Values may be sent and summed in bfloat16 or wider, within the bound.
A program may use at most 192 MiB of HBM per device.

```python
import math
import jax
import jax.numpy as jnp
from jax import lax

QUERY_HEADS = 128
KEY_VALUE_HEADS = 8
HEAD_SIZE = 128
F = 64
TOK_DEV = 128
SEQUENCE_TOKENS = 4096


def attention_pair(key):
    seed_query = jax.random.fold_in(key, 101)
    random_key_seeds = jax.random.fold_in(key, 202)
    queries = jnp.clip(2.0 * jax.random.normal(seed_query, (SEQUENCE_TOKENS, QUERY_HEADS, HEAD_SIZE), jnp.float32), -8.0, 8.0)
    key_row_vectors = jnp.clip(jax.random.normal(random_key_seeds, (SEQUENCE_TOKENS, KEY_VALUE_HEADS, HEAD_SIZE), jnp.float32), -4.0, 4.0)
    return (queries, key_row_vectors)


def draw_queries(key, part):
    return attention_pair(key)[0].astype(jnp.bfloat16)


def draw_key_states(key, part):
    return attention_pair(key)[1].astype(jnp.bfloat16)


def steps_of(stream_key, extent, shards, least, high):
    level, own = 1.0, jax.random.fold_in(stream_key, 6)
    for axis_at, parts in shards:
        draws = jnp.exp(jax.random.uniform(jax.random.fold_in(own, axis_at), (parts,), jnp.float32, least / len(shards), high / len(shards)))
        level = level * jnp.repeat(draws, extent[axis_at] // parts).reshape([-1 if axis == axis_at else 1 for axis in range(len(extent))])
    return level


def scatter_about(key, dims, width, reach, shards=(), held_as=jnp.bfloat16):
    drawn = width * jax.random.normal(key, dims, jnp.float32)
    if shards:
        drawn = drawn * steps_of(key, dims, shards, -0.22, 0.18)
    return jnp.clip(drawn, -reach, reach).astype(held_as)


def setup_inputs(seed: int = 0) -> dict:
    key_list = jax.random.split(jax.random.key(seed), 6)
    return {
        "queries": draw_queries(jax.random.fold_in(key_list[5], 71), 0),
        "key_states": draw_key_states(jax.random.fold_in(key_list[5], 71), 0),
        "value_vector_states": scatter_about(key_list[2], (SEQUENCE_TOKENS, KEY_VALUE_HEADS, HEAD_SIZE), 1.0, 6.0, ((0, 32), (1, 8))),
        "map_query": scatter_about(key_list[3], (QUERY_HEADS, HEAD_SIZE, F), HEAD_SIZE ** -0.5, 0.5, ((0, 8),), jnp.float32),
        "map_key": scatter_about(key_list[4], (QUERY_HEADS, HEAD_SIZE, F), HEAD_SIZE ** -0.5, 0.5, ((0, 8),), jnp.float32),
    }


HIGHEST = lax.Precision.HIGHEST

def feature(values):
    return jnp.concatenate([jax.nn.elu(values) + 1.0, jax.nn.elu(-values) + 1.0], axis=-1)

def teacher_rows(query_rows, key_row_vectors, value_rows):
    score_scale = 1.0 / math.sqrt(HEAD_SIZE)
    scores = jnp.dot(query_rows, key_row_vectors.T, precision=HIGHEST) * score_scale
    causal = jnp.arange(SEQUENCE_TOKENS, dtype=jnp.int32)[None, :] <= jnp.arange(SEQUENCE_TOKENS, dtype=jnp.int32)[:, None]
    scores = jnp.where(causal, scores, -1e+30)
    row_top = lax.optimization_barrier(jnp.max(scores, axis=1, keepdims=True))
    weights = jnp.where(causal, jnp.exp(scores - row_top), 0.0)
    row_total = lax.optimization_barrier(jnp.sum(weights, axis=1, keepdims=True))
    rounded = lax.optimization_barrier(weights.astype(jnp.bfloat16)).astype(jnp.float32)
    return jnp.dot(rounded, value_rows, precision=HIGHEST) / row_total

def head_error(weights, query_rows, key_row_vectors, value_rows, target):
    weight_query, weight_key = weights
    phi_query = feature(jnp.dot(query_rows, weight_query, precision=HIGHEST))
    phi_key = feature(jnp.dot(key_row_vectors, weight_key, precision=HIGHEST))
    blocks = SEQUENCE_TOKENS // TOK_DEV
    feature_width = phi_query.shape[1]
    causal = (jnp.arange(TOK_DEV, dtype=jnp.int32)[None, :] <= jnp.arange(TOK_DEV, dtype=jnp.int32)[:, None]).astype(jnp.float32)

    def advance(carried, inputs):
        state_sum, norm_sum = carried
        block_query, block_key, block_value, block_target = inputs
        inner_scores = jnp.dot(block_query, block_key.T, precision=HIGHEST) * causal
        numerator = jnp.dot(inner_scores, block_value, precision=HIGHEST) + jnp.dot(block_query, state_sum, precision=HIGHEST)
        denominator = lax.optimization_barrier(jnp.sum(inner_scores, axis=1)) + jnp.dot(block_query, norm_sum, precision=HIGHEST)
        student = numerator / denominator[:, None]
        state_sum = state_sum + jnp.dot(block_key.T, block_value, precision=HIGHEST)
        norm_sum = norm_sum + lax.optimization_barrier(jnp.sum(block_key, axis=0))
        mismatch = student - block_target
        return ((state_sum, norm_sum), jnp.sum(mismatch * mismatch))
    initial = (jnp.zeros((feature_width, HEAD_SIZE), jnp.float32), jnp.zeros((feature_width,), jnp.float32))
    stacked = (phi_query.reshape(blocks, TOK_DEV, feature_width), phi_key.reshape(blocks, TOK_DEV, feature_width), value_rows.reshape(blocks, TOK_DEV, HEAD_SIZE), target.reshape(blocks, TOK_DEV, HEAD_SIZE))
    last_state, errors = lax.scan(advance, initial, stacked)
    return jnp.sum(errors)

def reference(queries, key_states, value_vector_states, map_query, map_key):
    query_group_count = QUERY_HEADS // KEY_VALUE_HEADS
    query_major = jnp.transpose(queries.astype(jnp.float32), (1, 0, 2))
    key_major = jnp.transpose(key_states.astype(jnp.float32), (1, 0, 2))
    value_major = jnp.transpose(value_vector_states.astype(jnp.float32), (1, 0, 2))
    head_numbers = jnp.arange(QUERY_HEADS, dtype=jnp.int32)

    def teacher_head(inputs):
        query_rows, head_number = inputs
        group_index = (head_number // query_group_count).astype(jnp.int32)
        key_row_vectors = lax.dynamic_index_in_dim(key_major, group_index, 0, keepdims=False)
        value_rows = lax.dynamic_index_in_dim(value_major, group_index, 0, keepdims=False)
        return teacher_rows(query_rows, key_row_vectors, value_rows)
    teacher = lax.map(teacher_head, (query_major, head_numbers))
    energy = jnp.sum(teacher * teacher)

    def student_grad(inputs):
        query_rows, head_number, weight_query, weight_key, target = inputs
        group_index = (head_number // query_group_count).astype(jnp.int32)
        key_row_vectors = lax.dynamic_index_in_dim(key_major, group_index, 0, keepdims=False)
        value_rows = lax.dynamic_index_in_dim(value_major, group_index, 0, keepdims=False)
        return jax.grad(head_error)((weight_query, weight_key), query_rows, key_row_vectors, value_rows, target)
    grad_query, grad_key = lax.map(student_grad, (query_major, head_numbers, map_query, map_key, teacher))
    factor = QUERY_HEADS / energy
    return (grad_query * factor, grad_key * factor)
```

```python
import math

import jax
import jax.numpy as jnp
from jax import lax
from jax.experimental import pallas as pl
from jax.experimental.pallas import tpu as pltpu
from jax.sharding import Mesh
from jax.sharding import PartitionSpec as P

F32 = jnp.float32
BF16 = jnp.bfloat16
MESH = pl.DeviceIdType.MESH
HALF = 64
LOSS_SCALE = 256.0


def nn(a, b):
    return lax.dot_general(a, b, (((1,), (0,)), ((), ())), preferred_element_type=F32)


def nt(a, b):
    return lax.dot_general(a, b, (((1,), (1,)), ((), ())), preferred_element_type=F32)


def split(value):
    high = value.astype(BF16)
    return high, (value - high.astype(F32)).astype(BF16)


def rows(start, size):
    return pl.ds(pl.multiple_of(start, size), size)


def owner_of(chunk_x):
    return jnp.where((chunk_x == 0) | (chunk_x == 3), 0, 1)


def chunk_of(core, slot):
    return jnp.where(core == 0, jnp.where(slot < 4, slot, slot + 8), slot + 4)


def ring_steps(copy, place, a, b, on_arrival):
    A, B = place[a], place[b]

    def at(da, db):
        spot = dict(place)
        spot[a] = lax.rem(A + da + 4, 4)
        spot[b] = lax.rem(B + db + 4, 4)
        return spot

    up_a, down_a, up_b, down_b = at(1, 0), at(-1, 0), at(0, 1), at(0, -1)
    sent = []

    def send(origin, part, target, index):
        transfer = copy(origin, part, target, index)
        transfer.start()
        sent.append(transfer)

    def wait(origin, part, index):
        copy(origin, part, origin, index).wait_recv()

    def onward(da, d):
        send(at(da, 0), None, up_b, 4 + 4 * d)
        send(at(da, 0), None, down_b, 5 + 4 * d)

    def own():
        send(at(0, 0), None, up_a, 0)
        send(at(0, 0), None, down_a, 1)
        onward(0, 0)
        on_arrival(at(0, 0))

    def from_down_a():
        wait(at(-1, 0), None, 0)
        send(at(-1, 0), 0, up_a, 2)
        onward(-1, 1)
        on_arrival(at(-1, 0))

    def from_up_a():
        wait(at(1, 0), None, 1)
        send(at(1, 0), 1, down_a, 3)
        onward(1, 2)
        on_arrival(at(1, 0))

    def opposite_a():
        wait(at(2, 0), 0, 2)
        wait(at(2, 0), 1, 3)
        onward(2, 3)
        on_arrival(at(2, 0))

    steps = [own, from_down_a, from_up_a, opposite_a]
    for d, da in enumerate((0, -1, 1, 2)):

        def from_sides(d=d, da=da):
            wait(at(da, -1), None, 4 + 4 * d)
            send(at(da, -1), 0, up_b, 6 + 4 * d)
            on_arrival(at(da, -1))
            wait(at(da, 1), None, 5 + 4 * d)
            send(at(da, 1), 1, down_b, 7 + 4 * d)
            on_arrival(at(da, 1))

        steps.append(from_sides)
    for d, da in enumerate((0, -1, 1, 2)):

        def opposite_b(d=d, da=da):
            wait(at(da, 2), 0, 6 + 4 * d)
            wait(at(da, 2), 1, 7 + 4 * d)
            on_arrival(at(da, 2))

        steps.append(opposite_b)
    return steps, sent


def two_gathers(buffers, parts, place, my_core, ici_send, ici_recv, die_send, die_recv):
    other = dict(place)
    other["c"] = 1 - my_core
    all_steps, all_sent, handed = [], [], []
    for t, (a, b) in enumerate((("x", "y"), ("y", "x"))):

        def copy(origin, part, target, index, t=t):
            where = parts[t](origin, my_core, part)
            return pltpu.make_async_remote_copy(
                src_ref=buffers[t].at[where],
                dst_ref=buffers[t].at[where],
                send_sem=ici_send.at[t, index],
                recv_sem=ici_recv.at[t, index],
                device_id=target,
                device_id_type=MESH,
            )

        def hand_over(origin, t=t):
            chip = origin["x"] * 4 + origin["y"]
            where = parts[t](origin, my_core, None)
            transfer = pltpu.make_async_remote_copy(
                src_ref=buffers[t].at[where],
                dst_ref=buffers[t].at[where],
                send_sem=die_send.at[t, chip],
                recv_sem=die_recv.at[t, chip],
                device_id=other,
                device_id_type=MESH,
            )
            transfer.start()
            handed.append(transfer)

        base = {"x": place["x"], "y": place["y"], "c": my_core}
        steps, sent = ring_steps(copy, base, a, b, hand_over)
        all_steps.append(steps)
        all_sent.append(sent)
    for pair in zip(*all_steps):
        for step in pair:
            step()

    def wait_handed(t, chip):
        where = parts[t]({"x": chip // 4, "y": lax.rem(chip, 4)}, 1 - my_core, None)
        pltpu.make_async_remote_copy(
            src_ref=buffers[t].at[where],
            dst_ref=buffers[t].at[where],
            send_sem=die_send.at[t, chip],
            recv_sem=die_recv.at[t, chip],
            device_id=other,
            device_id_type=MESH,
        ).wait_recv()

    for t in range(2):
        for chip in range(16):
            wait_handed(t, chip)
    for sent in all_sent + [handed]:
        for transfer in sent:
            transfer.wait_send()


def kernel(
    q_hbm, k_hbm, v_hbm, wq_hbm, wk_hbm, out_ref,
    qbuf, kbuf, vext, vbuf, wq_t, wk_t, scores, acc, teacher_out,
    phi_hi, phi_lo, slope, state_hi, state_lo, carry, diag, back, mq, mk, energy,
    own_part, other_part, energies, gathered,
    q_send, q_recv, local_sem, ici_send, ici_recv, die_send, die_recv,
    out_send, out_recv, odie_send, odie_recv, pair_send, pair_recv, z_send, z_recv,
):
    x, y, core, z = (lax.axis_index(n) for n in ("x", "y", "c", "z"))
    chip = x * 4 + y
    mine = chip * 2 + core

    barrier = pltpu.get_barrier_semaphore()
    peers = 0
    for dx in range(4):
        for dy in range(4):
            for dc in range(2):
                if dx or dy or dc:
                    target = {"x": lax.rem(x + dx, 4), "y": lax.rem(y + dy, 4), "c": lax.rem(core + dc, 2)}
                    pl.semaphore_signal(barrier, inc=1, device_id=target, device_id_type=MESH)
                    peers += 1
    for dz in range(1, 8):
        pl.semaphore_signal(barrier, inc=1, device_id={"z": lax.rem(z + dz, 8)}, device_id_type=MESH)
        peers += 1

    local = [
        pltpu.make_async_copy(k_hbm, kbuf.at[rows(mine * 128, 128)], local_sem.at[0]),
        pltpu.make_async_copy(v_hbm, vbuf.at[rows(mine * 128, 128)], local_sem.at[1]),
        pltpu.make_async_copy(wq_hbm.at[chip], wq_t, local_sem.at[2]),
        pltpu.make_async_copy(wk_hbm.at[chip], wk_t, local_sem.at[3]),
    ]
    for c in local:
        c.start()
    for c in local:
        c.wait()
    pl.semaphore_wait(barrier, peers)

    target_core = owner_of(x)
    my_slot = jnp.where(x >= 2, 4, 0) + y
    q_rows = rows((my_slot * 2 + core) * 128, 128)
    q_index = my_slot * 2 + core

    def q_copy(r):
        head = lax.rem(chip + r, 16)
        return pltpu.make_async_remote_copy(
            src_ref=q_hbm.at[head],
            dst_ref=qbuf.at[q_rows],
            send_sem=q_send.at[r],
            recv_sem=q_recv.at[q_index],
            device_id={"x": head // 4, "y": lax.rem(head, 4), "c": target_core},
            device_id_type=MESH,
        )

    q_self = pltpu.make_async_copy(q_hbm.at[chip], qbuf.at[q_rows], local_sem.at[4])

    @pl.when(target_core == core)
    def _():
        q_self.start()

    @pl.when(target_core != core)
    def _():
        q_copy(0).start()

    for r in range(1, 16):
        q_copy(r).start()

    def block_rows(origin, c, part):
        start = ((origin["x"] * 4 + origin["y"]) * 2 + c) * 128
        if part is None:
            return rows(start, 128)
        return rows(start + part * 64, 64)

    place = {"x": x, "y": y}
    two_gathers((kbuf, vbuf), (block_rows, block_rows), place, core, ici_send, ici_recv, die_send, die_recv)

    @pl.when(target_core == core)
    def _():
        q_self.wait()

    @pl.when(target_core != core)
    def _():
        q_copy(0).wait_send()

    for r in range(1, 16):
        q_copy(r).wait_send()
    for slot in range(8):
        source = chunk_of(core, slot)
        for c in range(2):

            @pl.when((source != chip) | (core != c))
            def _(slot=slot, c=c):
                pltpu.make_async_remote_copy(
                    src_ref=q_hbm.at[0],
                    dst_ref=qbuf.at[pl.ds((slot * 2 + c) * 128, 128)],
                    send_sem=q_send.at[0],
                    recv_sem=q_recv.at[slot * 2 + c],
                    device_id={"c": core},
                    device_id_type=MESH,
                ).wait_recv()

    compute(
        core, qbuf, kbuf, vext, vbuf, wq_t, wk_t, scores, acc, teacher_out,
        phi_hi, phi_lo, slope, state_hi, state_lo, carry, diag, back, mq, mk, energy,
    )

    part_q = mq[0:64, :] - mq[64:128, :]
    part_k = mk[0:64, :] - mk[64:128, :]
    keep = jnp.where(core == 0, part_q, part_k)
    own_part[...] = jnp.where(core == 0, part_k, part_q)
    pair = pltpu.make_async_remote_copy(
        src_ref=own_part, dst_ref=other_part, send_sem=pair_send, recv_sem=pair_recv,
        device_id={"c": 1 - core}, device_id_type=MESH,
    )
    pair.start()
    z_copies = []
    for dz in range(1, 8):
        c = pltpu.make_async_remote_copy(
            src_ref=energy, dst_ref=energies.at[dz], send_sem=z_send.at[dz], recv_sem=z_recv.at[dz],
            device_id={"z": lax.rem(z + dz, 8)}, device_id_type=MESH,
        )
        c.start()
        z_copies.append(c)
    pair.wait()
    gathered[pl.ds(pl.multiple_of(mine * 72, 8), 64), :] = keep + other_part[...]
    total = energy[...]
    for dz in range(1, 8):
        z_copies[dz - 1].wait()
        total = total + energies[dz]
    gathered[pl.ds(pl.multiple_of(mine * 72 + 64, 8), 8), :] = total

    def upper(origin, c, part):
        start = ((origin["x"] * 4 + origin["y"]) * 2 + c) * 72
        first, size = {None: (0, 40), 0: (0, 16), 1: (16, 24)}[part]
        return pl.ds(pl.multiple_of(start + first, 8), size)

    def lower(origin, c, part):
        start = ((origin["x"] * 4 + origin["y"]) * 2 + c) * 72
        first, size = {None: (40, 32), 0: (40, 16), 1: (56, 16)}[part]
        return pl.ds(pl.multiple_of(start + first, 8), size)

    two_gathers((gathered, gathered), (upper, lower), place, core, out_send, out_recv, odie_send, odie_recv)
    done = pltpu.make_async_copy(gathered, out_ref, local_sem.at[5])
    done.start()
    done.wait()


def feature_parts(logit):
    slope = jnp.exp(jnp.minimum(logit, 0.0))
    return slope + jnp.maximum(logit, 0.0), slope


def compute(
    core, qbuf, kbuf, vext, vbuf, wq_t, wk_t, scores, acc, teacher_out,
    phi_hi, phi_lo, slope, state_hi, state_lo, carry, diag, back, mq, mk, energy,
):
    scale = math.log2(math.e) / math.sqrt(128.0)

    def signed(w_ref):
        hi, lo = split(jnp.concatenate([w_ref[...], -w_ref[...]], axis=0))
        return jnp.concatenate([hi, lo], axis=1)

    wq2 = signed(wq_t)
    wk2 = signed(wk_t)
    vext[:, 0:128] = vbuf[...]
    vext[:, 128:256] = jnp.ones((4096, 128), BF16)
    carry[...] = jnp.zeros_like(carry)
    mq[...] = jnp.zeros_like(mq)
    mk[...] = jnp.zeros_like(mk)
    energy[...] = jnp.zeros_like(energy)

    @pl.loop(0, 16)
    def _(j):
        keys = kbuf[rows(j * 256, 256), :]
        values = vext[rows(j * 256, 256), :]
        logit = nt(wk2, jnp.concatenate([keys, keys], axis=1))
        phi, s = feature_parts(logit)
        slope[j] = s
        hi, lo = split(phi)
        phi_hi[j] = hi
        phi_lo[j] = lo
        before = carry[...]
        sh, sl = split(before)
        state_hi[j] = sh
        state_lo[j] = sl
        carry[...] = before + nn(hi, values) + nn(lo, values)
        diag[j] = jnp.zeros((128, 256), F32)
        back[j] = jnp.zeros((128, 256), F32)

    @pl.loop(0, 8)
    def _(slot):
        chunk = chunk_of(core, slot)
        q = qbuf[rows(slot * 256, 256), :]
        last = chunk // 2

        def widest(s, top):
            for i in range(4):
                top = jnp.maximum(top, s[:, i * 128 : (i + 1) * 128])
            return top

        def score(jj, top):
            s = nt(q, kbuf[rows(jj * 512, 512), :])
            scores[jj] = s
            return widest(s, top)

        top = lax.fori_loop(0, last, score, jnp.full((256, 128), -1e30, F32))
        s = nt(q, kbuf[rows(last * 512, 512), :])
        row = lax.broadcasted_iota(jnp.int32, (256, 512), 0) + lax.rem(chunk, 2) * 256
        col = lax.broadcasted_iota(jnp.int32, (256, 512), 1)
        s = jnp.where(col <= row, s, -1e30)
        scores[last] = s
        top = jnp.max(widest(s, top), axis=1, keepdims=True) * scale
        acc[...] = jnp.zeros_like(acc)

        @pl.loop(0, last + 1)
        def _(jj):
            w = jnp.exp2(scores[jj] * scale - top).astype(BF16)
            acc[...] += nn(w, vext[rows(jj * 512, 512), :])

        t = acc[:, 0:128] / acc[:, 128:256]
        teacher_out[slot] = t
        energy[...] += jnp.sum((t * t).reshape(32, 8, 128), axis=0)

    @pl.loop(0, 8)
    def _(slot):
        chunk = chunk_of(core, slot)
        q = qbuf[rows(slot * 256, 256), :]
        values = vext[rows(chunk * 256, 256), :]
        q2 = jnp.concatenate([q, q], axis=1)
        phi, _ = feature_parts(nt(q2, wq2))
        phi_t, slope_t = feature_parts(nt(wq2, q2))
        qh, ql = split(phi)
        qth, qtl = split(phi_t)
        kh, kl = phi_hi[chunk], phi_lo[chunk]
        sh, sl = state_hi[chunk], state_lo[chunk]
        row = lax.broadcasted_iota(jnp.int32, (256, 256), 0)
        col = lax.broadcasted_iota(jnp.int32, (256, 256), 1)
        visible = col <= row
        inner = jnp.where(visible, nn(qh, kh) + nn(qh, kl) + nn(ql, kh), 0.0)
        ih, il = split(inner)
        both = nn(ih, values) + nn(il, values) + nn(qh, sh) + nn(qh, sl) + nn(ql, sh)
        inverse = 1.0 / both[:, 128:256]
        student = both[:, 0:128] * inverse
        grad_out = LOSS_SCALE * (student - teacher_out[slot])
        grad_numer = grad_out * inverse
        gh, gl = split(jnp.concatenate([grad_numer, -(grad_numer * student)], axis=1))
        grad_inner = jnp.where(visible, nt(gh, values) + nt(gl, values), 0.0)
        gih, gil = split(grad_inner)
        back[chunk] = nn(qth, gh) + nn(qth, gl) + nn(qtl, gh)
        diag[chunk] = nn(qth, gih) + nn(qth, gil) + nn(qtl, gih)
        grad_phi = (
            nt(kh, gih) + nt(kh, gil) + nt(kl, gih) + nt(sh, gh) + nt(sh, gl) + nt(sl, gh)
        )
        dh, dl = split(grad_phi * slope_t)
        mq[...] += nn(dh, q) + nn(dl, q)

    carry[...] = jnp.zeros_like(carry)

    @pl.loop(0, 16)
    def _(i):
        j = 15 - i
        keys = kbuf[rows(j * 256, 256), :]
        values = vext[rows(j * 256, 256), :]
        later = carry[...]
        lh, ll = split(later)
        grad_phi = nt(lh, values) + nt(ll, values) + diag[j]
        dh, dl = split(grad_phi * slope[j])
        mk[...] += nn(dh, keys) + nn(dl, keys)
        carry[...] = later + back[j]


def scratch():
    v = pltpu.VMEM
    return [
        v((2048, 128), BF16), v((4096, 128), BF16), v((4096, 256), BF16), v((4096, 128), BF16),
        v((64, 128), F32), v((64, 128), F32), v((8, 256, 512), F32), v((256, 256), F32),
        v((8, 256, 128), F32),
        v((16, 128, 256), BF16), v((16, 128, 256), BF16), v((16, 128, 256), F32),
        v((16, 128, 256), BF16), v((16, 128, 256), BF16), v((128, 256), F32),
        v((16, 128, 256), F32), v((16, 128, 256), F32), v((128, 128), F32), v((128, 128), F32),
        v((8, 128), F32),
        v((64, 128), F32), v((64, 128), F32), v((8, 8, 128), F32), v((32 * 72, 128), F32),
    ]


def semaphores():
    dma = pltpu.SemaphoreType.DMA
    return [
        dma((16,)), dma((16,)), dma((6,)), dma((2, 20)), dma((2, 20)), dma((2, 16)), dma((2, 16)),
        dma((2, 20)), dma((2, 20)), dma((2, 16)), dma((2, 16)), dma, dma, dma((8,)), dma((8,)),
    ]


def on_device(queries, key_states, value_vector_states, map_query, map_key):
    heads_first = jnp.transpose(queries, (1, 0, 2))
    any_space = pl.BlockSpec(memory_space=pl.ANY)
    gathered = pl.pallas_call(
        kernel,
        out_shape=jax.ShapeDtypeStruct((32 * 72, 128), F32),
        in_specs=[any_space] * 5,
        out_specs=any_space,
        scratch_shapes=scratch() + semaphores(),
        compiler_params=pltpu.CompilerParams(
            collective_id=0, has_side_effects=True, vmem_limit_bytes=60 * 1024 * 1024
        ),
        name="transfer_step",
    )(
        heads_first,
        key_states.reshape(128, 128),
        value_vector_states.reshape(128, 128),
        jnp.swapaxes(map_query, 1, 2),
        jnp.swapaxes(map_key, 1, 2),
    )
    blocks = gathered.reshape(16, 2, 72, 128)
    inverse = 1.0 / jnp.sum(blocks[:, :, 64:, :])
    grads = blocks[:, :, :64, :] * inverse
    return jnp.swapaxes(grads[:, 0], 1, 2), jnp.swapaxes(grads[:, 1], 1, 2)


def solution(mesh):
    torus = Mesh(mesh.devices.reshape(4, 4, 2, mesh.shape["head"]), ("x", "y", "c", "z"))
    ctx = ("x", "y", "c")
    in_specs = (
        P(ctx, "z", None),
        P(ctx, "z", None),
        P(ctx, "z", None),
        P("z", None, None),
        P("z", None, None),
    )
    out_specs = (P("z", None, None), P("z", None, None))
    return jax.shard_map(
        on_device, mesh=torus, in_specs=in_specs, out_specs=out_specs, check_vma=False
    )
```

```python
import math

import jax
import jax.numpy as jnp
from jax import lax
from jax.experimental import pallas as pl
from jax.experimental.pallas import tpu as pltpu
from jax.sharding import Mesh
from jax.sharding import PartitionSpec as P

F32 = jnp.float32
BF16 = jnp.bfloat16
MESH = pl.DeviceIdType.MESH
HALF = 64
LOSS_SCALE = 256.0


def nn(a, b):
    return lax.dot_general(a, b, (((1,), (0,)), ((), ())), preferred_element_type=F32)


def nt(a, b):
    return lax.dot_general(a, b, (((1,), (1,)), ((), ())), preferred_element_type=F32)


def split(value):
    high = value.astype(BF16)
    return high, (value - high.astype(F32)).astype(BF16)


def rows(start, size):
    return pl.ds(pl.multiple_of(start, size), size)


def owner_of(chunk_x):
    return jnp.where((chunk_x == 0) | (chunk_x == 3), 0, 1)


def chunk_of(core, slot):
    return jnp.where(core == 0, jnp.where(slot < 4, slot, slot + 8), slot + 4)


def ring_steps(copy, place, a, b, on_arrival, direct):
    A, B = place[a], place[b]

    def at(da, db):
        spot = dict(place)
        spot[a] = lax.rem(A + da + 4, 4)
        spot[b] = lax.rem(B + db + 4, 4)
        return spot

    up_a, down_a, up_b, down_b = at(1, 0), at(-1, 0), at(0, 1), at(0, -1)
    sent = []

    def send(origin, part, target, index):
        transfer = copy(origin, part, target, index)
        transfer.start()
        sent.append(transfer)

    def wait(origin, part, index):
        copy(origin, part, origin, index).wait_recv()

    def onward(da, d):
        send(at(da, 0), None, up_b, 4 + 4 * d)
        send(at(da, 0), None, down_b, 5 + 4 * d)
        if direct[1]:
            send(at(da, 0), None, at(0, 2), 6 + 4 * d)

    def own():
        send(at(0, 0), None, up_a, 0)
        send(at(0, 0), None, down_a, 1)
        if direct[0]:
            send(at(0, 0), None, at(2, 0), 2)
        onward(0, 0)
        on_arrival(at(0, 0))

    def from_down_a():
        wait(at(-1, 0), None, 0)
        if not direct[0]:
            send(at(-1, 0), 0, up_a, 2)
        onward(-1, 1)
        on_arrival(at(-1, 0))

    def from_up_a():
        wait(at(1, 0), None, 1)
        if not direct[0]:
            send(at(1, 0), 1, down_a, 3)
        onward(1, 2)
        on_arrival(at(1, 0))

    def opposite_a():
        if direct[0]:
            wait(at(2, 0), None, 2)
        else:
            wait(at(2, 0), 0, 2)
            wait(at(2, 0), 1, 3)
        onward(2, 3)
        on_arrival(at(2, 0))

    steps = [own, from_down_a, from_up_a, opposite_a]
    for d, da in enumerate((0, -1, 1, 2)):

        def from_sides(d=d, da=da):
            wait(at(da, -1), None, 4 + 4 * d)
            if not direct[1]:
                send(at(da, -1), 0, up_b, 6 + 4 * d)
            on_arrival(at(da, -1))
            wait(at(da, 1), None, 5 + 4 * d)
            if not direct[1]:
                send(at(da, 1), 1, down_b, 7 + 4 * d)
            on_arrival(at(da, 1))

        steps.append(from_sides)
    for d, da in enumerate((0, -1, 1, 2)):

        def opposite_b(d=d, da=da):
            if direct[1]:
                wait(at(da, 2), None, 6 + 4 * d)
            else:
                wait(at(da, 2), 0, 6 + 4 * d)
                wait(at(da, 2), 1, 7 + 4 * d)
            on_arrival(at(da, 2))

        steps.append(opposite_b)
    return steps, sent


class TwoGathers:
    def __init__(self, buffers, parts, place, core, sems, direct):
        self.buffers, self.parts, self.core = buffers, parts, core
        self.ici_send, self.ici_recv, self.die_send, self.die_recv = sems
        self.sent, self.handed, steps = [], [], []
        base = {"x": place["x"], "y": place["y"], "c": core}
        for t, (a, b) in enumerate((("x", "y"), ("y", "x"))):
            found, sent = ring_steps(
                lambda origin, part, target, index, t=t: self.copy(t, origin, part, target, index),
                base, a, b, lambda origin, t=t: self.hand_over(t, origin), direct,
            )
            steps.append(found)
            self.sent.append(sent)
        self.steps = list(zip(*steps))

    def copy(self, t, origin, part, target, index):
        where = self.parts[t](origin, self.core, part)
        return pltpu.make_async_remote_copy(
            src_ref=self.buffers[t].at[where],
            dst_ref=self.buffers[t].at[where],
            send_sem=self.ici_send.at[t, index],
            recv_sem=self.ici_recv.at[t, index],
            device_id=target,
            device_id_type=MESH,
        )

    def between_cores(self, t, origin, core):
        chip = origin["x"] * 4 + origin["y"]
        where = self.parts[t](origin, core, None)
        return pltpu.make_async_remote_copy(
            src_ref=self.buffers[t].at[where],
            dst_ref=self.buffers[t].at[where],
            send_sem=self.die_send.at[t, chip],
            recv_sem=self.die_recv.at[t, chip],
            device_id={"c": 1 - self.core},
            device_id_type=MESH,
        )

    def hand_over(self, t, origin):
        transfer = self.between_cores(t, origin, self.core)
        transfer.start()
        self.handed.append(transfer)

    def step(self, number):
        for part in self.steps[number]:
            part()

    def wait_handed(self, x, y):
        for t in range(2):
            self.between_cores(t, {"x": x, "y": y}, 1 - self.core).wait_recv()

    def wait_sent(self):
        for transfer in self.sent[0] + self.sent[1] + self.handed:
            transfer.wait_send()


READY = {
    1: ((0, 0),),
    5: ((-1, 0), (1, 0), (0, -1), (0, 1)),
    7: ((-1, -1), (1, 1), (-1, 1), (1, -1)),
    9: ((2, 0), (0, 2)),
    11: ((2, -1), (-1, 2), (2, 1), (1, 2), (2, 2)),
}
Q_SENDS = {0: 4, 1: 1, 2: 1, 3: 2, 4: 1, 5: 1, 6: 1, 7: 1, 8: 1, 9: 1, 10: 1, 11: 0}


def kernel(
    q_hbm, k_hbm, v_hbm, wq_hbm, wk_hbm, out_q, out_k,
    qbuf, kbuf, vext, vbuf, wq_t, wk_t, scores, acc, peak, teacher_out,
    phi_hi, phi_lo, slope, state, state_hi, state_lo, carry, diag, back, mq, mk, energy,
    part_q, part_k, other_q, other_k, energies, all_q, all_k,
    q_send, q_recv, local_sem, ici_send, ici_recv, die_send, die_recv,
    a_send, a_recv, a_die_send, a_die_recv, b_send, b_recv, b_die_send, b_die_recv,
    pair_send, pair_recv, z_send, z_recv,
):
    x, y, core, z = (lax.axis_index(n) for n in ("x", "y", "c", "z"))
    chip = x * 4 + y
    mine = chip * 2 + core
    place = {"x": x, "y": y}

    local = [
        pltpu.make_async_copy(k_hbm, kbuf.at[rows(mine * 128, 128)], local_sem.at[0]),
        pltpu.make_async_copy(v_hbm, vbuf.at[rows(mine * 128, 128)], local_sem.at[1]),
        pltpu.make_async_copy(wq_hbm.at[chip], wq_t, local_sem.at[2]),
        pltpu.make_async_copy(wk_hbm.at[chip], wk_t, local_sem.at[3]),
    ]
    for c in local:
        c.start()
    barrier = pltpu.get_barrier_semaphore()
    peers = 0
    for dx in range(4):
        for dy in range(4):
            for dc in range(2):
                if dx or dy or dc:
                    target = {"x": lax.rem(x + dx, 4), "y": lax.rem(y + dy, 4), "c": lax.rem(core + dc, 2)}
                    pl.semaphore_signal(barrier, inc=1, device_id=target, device_id_type=MESH)
                    peers += 1
    for dz in range(1, 8):
        pl.semaphore_signal(barrier, inc=1, device_id={"z": lax.rem(z + dz, 8)}, device_id_type=MESH)
        peers += 1
    vext[:, 128:256] = jnp.ones((4096, 128), BF16)
    diag[...] = jnp.zeros_like(diag)
    back[...] = jnp.zeros_like(back)
    for c in local:
        c.wait()
    pl.semaphore_wait(barrier, peers)

    target_core = owner_of(x)
    my_slot = jnp.where(x >= 2, 4, 0) + y
    q_rows = rows((my_slot * 2 + core) * 128, 128)
    q_index = my_slot * 2 + core

    def q_copy(r):
        head = lax.rem(chip + r, 16)
        return pltpu.make_async_remote_copy(
            src_ref=q_hbm.at[head],
            dst_ref=qbuf.at[q_rows],
            send_sem=q_send.at[r],
            recv_sem=q_recv.at[q_index],
            device_id={"x": head // 4, "y": lax.rem(head, 4), "c": target_core},
            device_id_type=MESH,
        )

    q_self = pltpu.make_async_copy(q_hbm.at[chip], qbuf.at[q_rows], local_sem.at[4])

    def block_rows(origin, c, part):
        start = ((origin["x"] * 4 + origin["y"]) * 2 + c) * 128
        if part is None:
            return rows(start, 128)
        return rows(start + part * 64, 64)

    gather = TwoGathers(
        (kbuf, vbuf), (block_rows, block_rows), place, core,
        (ici_send, ici_recv, die_send, die_recv), KV_DIRECT,
    )
    wk2 = signed(wk_t)
    q_next = 1
    for number in range(12):
        gather.step(number)
        if number == 0:

            @pl.when(target_core == core)
            def _():
                q_self.start()

            @pl.when(target_core != core)
            def _():
                q_copy(0).start()

        for _ in range(Q_SENDS[number]):
            q_copy(q_next).start()
            q_next += 1
        if number in READY:
            chunks = []
            for dx, dy in READY[number]:
                cx, cy = lax.rem(x + dx + 4, 4), lax.rem(y + dy + 4, 4)
                gather.wait_handed(cx, cy)
                chunks.append(cx * 4 + cy)
            for j in chunks:
                key_chunk(j, wk2, kbuf, vbuf, vext, phi_hi, phi_lo, slope, state)
    assert q_next == 16
    states(carry, state, state_hi, state_lo)

    for slot in range(8):
        source = chunk_of(core, slot)
        for c in range(2):

            @pl.when((source != chip) | (core != c))
            def _(slot=slot, c=c):
                pltpu.make_async_remote_copy(
                    src_ref=q_hbm.at[0],
                    dst_ref=qbuf.at[pl.ds((slot * 2 + c) * 128, 128)],
                    send_sem=q_send.at[0],
                    recv_sem=q_recv.at[slot * 2 + c],
                    device_id={"c": core},
                    device_id_type=MESH,
                ).wait_recv()

    @pl.when(target_core == core)
    def _():
        q_self.wait()

    teacher(core, qbuf, kbuf, vext, scores, acc, peak, teacher_out, energy)

    z_copies = []
    for dz in range(1, 8):
        c = pltpu.make_async_remote_copy(
            src_ref=energy, dst_ref=energies.at[dz], send_sem=z_send.at[dz], recv_sem=z_recv.at[dz],
            device_id={"z": lax.rem(z + dz, 8)}, device_id_type=MESH,
        )
        c.start()
        z_copies.append(c)

    student(
        core, qbuf, vext, wq_t, teacher_out, phi_hi, phi_lo, state_hi, state_lo, diag, back, mq
    )

    def swap(m, part, other, number):
        upper = m[0:32, :] - m[64:96, :]
        lower = m[32:64, :] - m[96:128, :]
        part[...] = jnp.where(core == 0, lower, upper)
        transfer = pltpu.make_async_remote_copy(
            src_ref=part, dst_ref=other, send_sem=pair_send.at[number], recv_sem=pair_recv.at[number],
            device_id={"c": 1 - core}, device_id_type=MESH,
        )
        transfer.start()
        return jnp.where(core == 0, upper, lower), transfer

    kept, pair = swap(mq, part_q, other_q, 0)

    def halves(size, at, first, second):
        def where(origin, c, part):
            start = ((origin["x"] * 4 + origin["y"]) * 2 + c) * size + at
            begin, length = {None: (0, first + second), 0: (0, first), 1: (first, second)}[part]
            return pl.ds(pl.multiple_of(start + begin, 8), length)

        return where

    gather_q = TwoGathers(
        (all_q, all_q), (halves(40, 0, 8, 16), halves(40, 24, 8, 8)), place, core,
        (a_send, a_recv, a_die_send, a_die_recv), OUT_DIRECT,
    )
    gather_k = TwoGathers(
        (all_k, all_k), (halves(32, 0, 8, 8), halves(32, 16, 8, 8)), place, core,
        (b_send, b_recv, b_die_send, b_die_recv), OUT_DIRECT,
    )
    mk[...] = jnp.zeros_like(mk)
    carry[...] = jnp.zeros_like(carry)
    key_backward(0, kbuf, vext, slope, carry, diag, back, mk)
    pair.wait_recv()
    all_q[pl.ds(pl.multiple_of(mine * 40, 8), 32), :] = kept + other_q[...]
    total = energy[...]
    for dz in range(1, 8):
        z_copies[dz - 1].wait_recv()
        total = total + energies[dz]
    all_q[pl.ds(pl.multiple_of(mine * 40 + 32, 8), 8), :] = total
    gather_q.step(0)
    key_backward(1, kbuf, vext, slope, carry, diag, back, mk)
    gather_q.step(1)
    gather_q.step(2)
    key_backward(2, kbuf, vext, slope, carry, diag, back, mk)
    gather_q.step(3)
    key_backward(3, kbuf, vext, slope, carry, diag, back, mk)
    kept_k, pair_k = swap(mk, part_k, other_k, 1)
    gather_q.step(4)
    pair_k.wait_recv()
    all_k[pl.ds(pl.multiple_of(mine * 32, 8), 32), :] = kept_k + other_k[...]
    gather_k.step(0)
    for number in range(5, 12):
        gather_q.step(number)
        gather_k.step(number - 4)
    for number in range(8, 12):
        gather_k.step(number)
    for cx in range(4):
        for cy in range(4):
            gather_q.wait_handed(cx, cy)
    tiles = [all_q[d * 40 + 32 : d * 40 + 40, :] for d in range(32)]
    while len(tiles) > 1:
        tiles = [p + q for p, q in zip(tiles[0::2], tiles[1::2])]
    sums = jnp.sum(jnp.sum(tiles[0], axis=0, keepdims=True), axis=1, keepdims=True)
    inverse = 1.0 / sums
    for d in range(32):
        out_q[d // 2, (d % 2) * 32 : (d % 2) * 32 + 32, :] = all_q[d * 40 : d * 40 + 32, :] * inverse
    for cx in range(4):
        for cy in range(4):
            gather_k.wait_handed(cx, cy)
    for d in range(32):
        out_k[d // 2, (d % 2) * 32 : (d % 2) * 32 + 32, :] = all_k[d * 32 : d * 32 + 32, :] * inverse

    @pl.when(target_core != core)
    def _():
        q_copy(0).wait_send()

    for r in range(1, 16):
        q_copy(r).wait_send()
    for c in z_copies + [pair, pair_k]:
        c.wait_send()
    for g in (gather, gather_q, gather_k):
        g.wait_sent()


KV_DIRECT = (True, False)
OUT_DIRECT = (True, True)


def feature_parts(logit):
    slope = jnp.exp(jnp.minimum(logit, 0.0))
    return slope + jnp.maximum(logit, 0.0), slope


def signed(w_ref):
    hi, lo = split(jnp.concatenate([w_ref[...], -w_ref[...]], axis=0))
    return jnp.concatenate([hi, lo], axis=1)


def key_chunk(j, wk2, kbuf, vbuf, vext, phi_hi, phi_lo, slope, state):
    keys = kbuf[rows(j * 256, 256), :]
    values = vbuf[rows(j * 256, 256), :]
    vext[rows(j * 256, 256), 0:128] = values
    values = jnp.concatenate([values, jnp.ones((256, 128), BF16)], axis=1)
    phi, s = feature_parts(nt(wk2, jnp.concatenate([keys, keys], axis=1)))
    slope[j] = s
    hi, lo = split(phi)
    phi_hi[j] = hi
    phi_lo[j] = lo
    both = nn(jnp.concatenate([hi, lo], axis=0), values)
    state[j] = both[0:128] + both[128:256]


def states(carry, state, state_hi, state_lo):
    carry[...] = jnp.zeros_like(carry)

    @pl.loop(0, 16)
    def _(j):
        before = carry[...]
        hi, lo = split(before)
        state_hi[j] = hi
        state_lo[j] = lo
        carry[...] = before + state[j]


def teacher(core, qbuf, kbuf, vext, scores, acc, peak, teacher_out, energy):
    scale = math.log2(math.e) / math.sqrt(128.0)
    energy[...] = jnp.zeros_like(energy)

    @pl.loop(0, 4)
    def _(pair):
        chunk = chunk_of(core, 2 * pair)
        q = qbuf[rows(pair * 512, 512), :]
        last = chunk // 2

        def widest(s, top):
            for i in range(4):
                top = jnp.maximum(top, s[:, i * 128 : (i + 1) * 128])
            return top

        peak[...] = jnp.full((512, 128), -1e30, F32)

        @pl.loop(0, last)
        def _(jj):
            s = nt(q, kbuf[rows(jj * 512, 512), :]) * scale
            scores[jj] = s
            peak[...] = widest(s, peak[...])

        s = nt(q, kbuf[rows(last * 512, 512), :]) * scale
        row = lax.broadcasted_iota(jnp.int32, (512, 512), 0)
        col = lax.broadcasted_iota(jnp.int32, (512, 512), 1)
        s = jnp.where(col <= row, s, -1e30)
        scores[last] = s
        peak[...] = jnp.broadcast_to(
            jnp.max(widest(s, peak[...]), axis=1, keepdims=True), (512, 128)
        )
        acc[...] = jnp.zeros_like(acc)

        @pl.loop(0, last + 1)
        def _(jj):
            for i in range(2):
                top = peak[...]
                w = [
                    jnp.exp2(scores[jj, :, (2 * i + h) * 128 : (2 * i + h + 1) * 128] - top)
                    for h in range(2)
                ]
                w = jnp.concatenate(w, axis=1).astype(BF16)
                acc[...] += nn(w, vext[rows(jj * 512 + i * 256, 256), :])

        t = acc[:, 0:128] / acc[:, 128:256]
        teacher_out[2 * pair] = t[0:256]
        teacher_out[2 * pair + 1] = t[256:512]
        energy[...] += jnp.sum((t * t).reshape(64, 8, 128), axis=0)


def student(
    core, qbuf, vext, wq_t, teacher_out, phi_hi, phi_lo, state_hi, state_lo, diag, back, mq
):
    wq2 = signed(wq_t)
    mq[...] = jnp.zeros_like(mq)
    row = lax.broadcasted_iota(jnp.int32, (256, 256), 0)
    col = lax.broadcasted_iota(jnp.int32, (256, 256), 1)
    visible = col <= row

    def one(slot):
        chunk = chunk_of(core, slot)
        q = qbuf[rows(slot * 256, 256), :]
        values = vext[rows(chunk * 256, 256), :]
        q2 = jnp.concatenate([q, q], axis=1)
        phi, _ = feature_parts(nt(q2, wq2))
        phi_t, slope_t = feature_parts(nt(wq2, q2))
        qh, ql = split(phi)
        qth, qtl = split(phi_t)
        qhh = jnp.concatenate([qh, qh], axis=1)
        qts = jnp.concatenate([qth, qtl], axis=0)
        kh, kl = phi_hi[chunk], phi_lo[chunk]
        sh, sl = state_hi[chunk], state_lo[chunk]
        ks = jnp.concatenate([kh, kl], axis=0)
        ss = jnp.concatenate([sh, sl], axis=0)
        inner = jnp.where(visible, nn(qhh, ks) + nn(ql, kh), 0.0)
        ih, il = split(inner)
        both = (nn(ih, values) + nn(il, values)) + (nn(qhh, ss) + nn(ql, sh))
        inverse = 1.0 / both[:, 128:256]
        student = both[:, 0:128] * inverse
        grad_out = LOSS_SCALE * (student - teacher_out[slot])
        grad_numer = grad_out * inverse
        gh, gl = split(jnp.concatenate([grad_numer, -(grad_numer * student)], axis=1))
        grad_inner = jnp.where(visible, nt(gh, values) + nt(gl, values), 0.0)
        gih, gil = split(grad_inner)
        back_both = nn(qts, gh)
        back[chunk] = (back_both[0:128] + back_both[128:256]) + nn(qth, gl)
        diag_both = nn(qts, gih)
        diag[chunk] = (diag_both[0:128] + diag_both[128:256]) + nn(qth, gil)
        grad_both = nt(ks, gih) + nt(ss, gh)
        grad_phi = (grad_both[0:128] + grad_both[128:256]) + (nt(kh, gil) + nt(sh, gl))
        dh, dl = split(grad_phi * slope_t)
        m_both = nn(jnp.concatenate([dh, dl], axis=0), q)
        return m_both[0:128] + m_both[128:256]

    @pl.loop(0, 8 // STUDENT_UNROLL)
    def _(step):
        parts = [one(step * STUDENT_UNROLL + h) for h in range(STUDENT_UNROLL)]
        mq[...] += sum(parts[1:], parts[0])


STUDENT_UNROLL = 2


def key_backward(group, kbuf, vext, slope, carry, diag, back, mk):
    later = carry[...]
    total = mk[...]
    for i in range(4):
        j = 15 - (group * 4 + i)
        keys = kbuf[rows(j * 256, 256), :]
        values = vext[rows(j * 256, 256), :]
        lh, ll = split(later)
        g_both = nt(jnp.concatenate([lh, ll], axis=0), values)
        grad_phi = (g_both[0:128] + g_both[128:256]) + diag[j]
        dh, dl = split(grad_phi * slope[j])
        m_both = nn(jnp.concatenate([dh, dl], axis=0), keys)
        total = total + (m_both[0:128] + m_both[128:256])
        later = later + back[j]
    mk[...] = total
    carry[...] = later


def scratch():
    v = pltpu.VMEM
    return [
        v((2048, 128), BF16), v((4096, 128), BF16), v((4096, 256), BF16), v((4096, 128), BF16),
        v((64, 128), F32), v((64, 128), F32), v((8, 512, 512), F32), v((512, 256), F32),
        v((512, 128), F32), v((8, 256, 128), F32),
        v((16, 128, 256), BF16), v((16, 128, 256), BF16), v((16, 128, 256), F32),
        v((16, 128, 256), F32), v((16, 128, 256), BF16), v((16, 128, 256), BF16), v((128, 256), F32),
        v((16, 128, 256), F32), v((16, 128, 256), F32), v((128, 128), F32), v((128, 128), F32),
        v((8, 128), F32),
    ]


def exchange_scratch():
    v, dma = pltpu.VMEM, pltpu.SemaphoreType.DMA
    return [
        v((32, 128), F32), v((32, 128), F32), v((32, 128), F32), v((32, 128), F32),
        v((8, 8, 128), F32), v((32 * 40, 128), F32), v((32 * 32, 128), F32),
        dma((16,)), dma((16,)), dma((6,)),
        dma((2, 20)), dma((2, 20)), dma((2, 16)), dma((2, 16)),
        dma((2, 20)), dma((2, 20)), dma((2, 16)), dma((2, 16)),
        dma((2, 20)), dma((2, 20)), dma((2, 16)), dma((2, 16)),
        dma((2,)), dma((2,)), dma((8,)), dma((8,)),
    ]


def on_device(queries, key_states, value_vector_states, map_query, map_key):
    heads_first = jnp.transpose(queries, (1, 0, 2))
    any_space = pl.BlockSpec(memory_space=pl.ANY)
    whole = pl.BlockSpec(memory_space=pltpu.VMEM)
    grad_query, grad_key = pl.pallas_call(
        kernel,
        out_shape=(jax.ShapeDtypeStruct((16, 64, 128), F32),) * 2,
        in_specs=[any_space] * 5,
        out_specs=(whole, whole),
        scratch_shapes=scratch() + exchange_scratch(),
        compiler_params=pltpu.CompilerParams(
            collective_id=0, has_side_effects=True, vmem_limit_bytes=60 * 1024 * 1024
        ),
        name="transfer_step",
    )(
        heads_first,
        key_states.reshape(128, 128),
        value_vector_states.reshape(128, 128),
        jnp.swapaxes(map_query, 1, 2),
        jnp.swapaxes(map_key, 1, 2),
    )
    return jnp.swapaxes(grad_query, 1, 2), jnp.swapaxes(grad_key, 1, 2)


def solution(mesh):
    torus = Mesh(mesh.devices.reshape(4, 4, 2, mesh.shape["head"]), ("x", "y", "c", "z"))
    ctx = ("x", "y", "c")
    in_specs = (
        P(ctx, "z", None),
        P(ctx, "z", None),
        P(ctx, "z", None),
        P("z", None, None),
        P("z", None, None),
    )
    out_specs = (P("z", None, None), P("z", None, None))
    return jax.shard_map(
        on_device, mesh=torus, in_specs=in_specs, out_specs=out_specs, check_vma=False
    )
```

```python
import math

import jax
import jax.numpy as jnp
from jax import lax
from jax.experimental import pallas as pl
from jax.experimental.pallas import tpu as pltpu
from jax.sharding import Mesh
from jax.sharding import PartitionSpec as P

F32 = jnp.float32
BF16 = jnp.bfloat16
MESH = pl.DeviceIdType.MESH
HALF = 64
LOSS_SCALE = 256.0


def nn(a, b):
    return lax.dot_general(a, b, (((1,), (0,)), ((), ())), preferred_element_type=F32)


def nt(a, b):
    return lax.dot_general(a, b, (((1,), (1,)), ((), ())), preferred_element_type=F32)


def split(value):
    high = value.astype(BF16)
    return high, (value - high.astype(F32)).astype(BF16)


def rows(start, size):
    return pl.ds(pl.multiple_of(start, size), size)


def owner_of(chunk_x):
    return jnp.where((chunk_x == 0) | (chunk_x == 3), 0, 1)


def chunk_of(core, slot):
    return jnp.where(core == 0, jnp.where(slot < 4, slot, slot + 8), slot + 4)


class Gather:
    def __init__(self, buffer, size, place, core, a, b, sems):
        self.buffer, self.size, self.place, self.core, self.a, self.b = buffer, size, place, core, a, b
        self.send_sem, self.recv_sem, self.die_send, self.die_recv = sems
        self.sent = []

    def first_row(self, core, at_b, at_a):
        return ((core * 4 + at_b) * 4 + at_a) * self.size

    def copy(self, start, count, target, sem, send_sem, recv_sem):
        where = pl.ds(pl.multiple_of(start, 8), count * self.size)
        return pltpu.make_async_remote_copy(
            src_ref=self.buffer.at[where],
            dst_ref=self.buffer.at[where],
            send_sem=send_sem.at[sem],
            recv_sem=recv_sem.at[sem],
            device_id=target,
            device_id_type=MESH,
        )

    def send(self, *args):
        transfer = self.copy(*args)
        transfer.start()
        self.sent.append(transfer)

    def start(self):
        here_a, here_b = self.place[self.a], self.place[self.b]
        for i, off in enumerate(OFFSETS):
            self.send(
                self.first_row(self.core, here_b, here_a), 1, {self.a: lax.rem(here_a + off, 4)},
                i, self.send_sem, self.recv_sem,
            )

    def second(self):
        here_a, here_b = self.place[self.a], self.place[self.b]
        for i, off in enumerate(OFFSETS):
            self.copy(
                self.first_row(self.core, here_b, lax.rem(here_a + 4 - off, 4)), 1,
                {self.a: here_a}, i, self.send_sem, self.recv_sem,
            ).wait_recv()
        for i, off in enumerate(OFFSETS):
            self.send(
                self.first_row(self.core, here_b, 0), 4, {self.b: lax.rem(here_b + off, 4)},
                3 + i, self.send_sem, self.recv_sem,
            )
        self.hand_over(3, 0)

    def hand_over(self, i, off):
        at_b = lax.rem(self.place[self.b] + 4 - off, 4)
        self.send(
            self.first_row(self.core, at_b, 0), 4, {"c": 1 - self.core}, i, self.die_send, self.die_recv
        )

    def third(self, i):
        at_b = lax.rem(self.place[self.b] + 4 - OFFSETS[i], 4)
        self.copy(
            self.first_row(self.core, at_b, 0), 4, {self.b: at_b}, 3 + i, self.send_sem, self.recv_sem
        ).wait_recv()
        self.hand_over(i, OFFSETS[i])

    def wait_handed(self, i):
        off = OFFSETS[i] if i < 3 else 0
        at_b = lax.rem(self.place[self.b] + 4 - off, 4)
        self.copy(
            self.first_row(1 - self.core, at_b, 0), 4, {"c": 1 - self.core}, i, self.die_send, self.die_recv
        ).wait_recv()
        return at_b

    def wait_sent(self):
        for transfer in self.sent:
            transfer.wait_send()


OFFSETS = (1, 3, 2)


def kernel(
    q_hbm, k_hbm, v_hbm, wq_hbm, wk_hbm, out_q, out_k, q_raw, q_wide, q_heads,
    qbuf, kbuf, kin, vext, vbuf, wq_t, wk_t, scores, acc, peak, teacher_out,
    phi_hi, phi_lo, slope, state_hi, state_lo, carry, diag, back, mq, mk, energy,
    part_q, part_k, other_q, other_k, energies, all_q, all_k,
    q_send, q_recv, local_sem, ici_send, ici_recv, die_send, die_recv,
    v_send, v_recv, v_die_send, v_die_recv,
    a_send, a_recv, a_die_send, a_die_recv, b_send, b_recv, b_die_send, b_die_recv,
    pair_send, pair_recv, z_send, z_recv,
):
    x, y, core, z = (lax.axis_index(n) for n in ("x", "y", "c", "z"))
    chip = x * 4 + y
    place = {"x": x, "y": y}

    local = [
        pltpu.make_async_copy(k_hbm, kin.at[rows((core * 16 + y * 4 + x) * 128, 128)], local_sem.at[0]),
        pltpu.make_async_copy(v_hbm, vbuf.at[rows((core * 16 + chip) * 128, 128)], local_sem.at[1]),
        pltpu.make_async_copy(wq_hbm.at[chip], wq_t, local_sem.at[2]),
        pltpu.make_async_copy(wk_hbm.at[chip], wk_t, local_sem.at[3]),
        pltpu.make_async_copy(q_hbm, q_raw, local_sem.at[5]),
    ]
    for c in local:
        c.start()
    barrier = pltpu.get_barrier_semaphore()
    peers = 0
    for dx in range(4):
        for dy in range(4):
            for dc in range(2):
                if dx or dy or dc:
                    target = {"x": lax.rem(x + dx, 4), "y": lax.rem(y + dy, 4), "c": lax.rem(core + dc, 2)}
                    pl.semaphore_signal(barrier, inc=1, device_id=target, device_id_type=MESH)
                    peers += 1
    for dz in range(1, 8):
        pl.semaphore_signal(barrier, inc=1, device_id={"z": lax.rem(z + dz, 8)}, device_id_type=MESH)
        peers += 1
    vext[:, 128:256] = jnp.ones((4096, 128), BF16)
    diag[...] = jnp.zeros_like(diag)
    back[...] = jnp.zeros_like(back)
    for c in local:
        c.wait()
    q_wide[...] = q_raw[...].astype(F32)
    for head in range(16):
        q_heads[head] = q_wide[pl.ds(head, 128, stride=16), :].astype(BF16)
    pl.semaphore_wait(barrier, peers)

    target_core = owner_of(x)
    my_slot = jnp.where(x >= 2, 4, 0) + y
    q_rows = rows((my_slot * 2 + core) * 128, 128)
    q_index = my_slot * 2 + core

    def q_copy(r):
        head = lax.rem(chip + r, 16)
        return pltpu.make_async_remote_copy(
            src_ref=q_heads.at[head],
            dst_ref=qbuf.at[q_rows],
            send_sem=q_send.at[r],
            recv_sem=q_recv.at[q_index],
            device_id={"x": head // 4, "y": lax.rem(head, 4), "c": target_core},
            device_id_type=MESH,
        )

    q_self = pltpu.make_async_copy(q_heads.at[chip], qbuf.at[q_rows], local_sem.at[4])

    gather_keys = Gather(
        kin, 128, place, core, "x", "y", (ici_send, ici_recv, die_send, die_recv)
    )
    gather_values = Gather(
        vbuf, 128, place, core, "y", "x", (v_send, v_recv, v_die_send, v_die_recv)
    )
    sent_queries = [0]

    def send_queries(count):
        for _ in range(count):
            sent_queries[0] += 1
            q_copy(sent_queries[0]).start()

    wk2 = signed(wk_t)
    gather_keys.start()

    @pl.when(target_core == core)
    def _():
        q_self.start()

    @pl.when(target_core != core)
    def _():
        q_copy(0).start()

    send_queries(Q_EARLY)
    if V_EARLY:
        gather_values.start()
    gather_keys.second()
    send_queries(15 - Q_EARLY)
    if not V_EARLY:
        gather_values.start()
    gather_values.second()
    for i in range(3):
        gather_keys.third(i)
    for i in (3, 0, 1, 2):
        key_features(gather_keys.wait_handed(i), wk2, kin, kbuf, phi_hi, phi_lo, slope)

    for slot in range(8):
        source = chunk_of(core, slot)
        for c in range(2):

            @pl.when((source != chip) | (core != c))
            def _(slot=slot, c=c):
                pltpu.make_async_remote_copy(
                    src_ref=q_heads.at[0],
                    dst_ref=qbuf.at[pl.ds((slot * 2 + c) * 128, 128)],
                    send_sem=q_send.at[0],
                    recv_sem=q_recv.at[slot * 2 + c],
                    device_id={"c": core},
                    device_id_type=MESH,
                ).wait_recv()

    @pl.when(target_core == core)
    def _():
        q_self.wait()

    for pair in range(4):
        teacher_scores(pair, core, qbuf, kbuf, scores, peak)
        if pair < 3:
            gather_values.third(pair)
    for i in (3, 0, 1, 2):
        gather_values.wait_handed(i)
    for c in range(2):
        for j in range(16):
            vext[j * 256 + c * 128 : j * 256 + c * 128 + 128, 0:128] = vbuf[
                (c * 16 + j) * 128 : (c * 16 + j + 1) * 128, :
            ]
    states(vext, phi_hi, phi_lo, carry, state_hi, state_lo)
    energy[...] = jnp.zeros_like(energy)
    for pair in range(4):
        teacher_weights(pair, core, vext, scores, peak, acc, teacher_out, energy)

    z_copies = []
    for dz in range(1, 8):
        c = pltpu.make_async_remote_copy(
            src_ref=energy, dst_ref=energies.at[dz], send_sem=z_send.at[dz], recv_sem=z_recv.at[dz],
            device_id={"z": lax.rem(z + dz, 8)}, device_id_type=MESH,
        )
        c.start()
        z_copies.append(c)

    student(
        core, qbuf, vext, wq_t, teacher_out, phi_hi, phi_lo, state_hi, state_lo, diag, back, mq
    )

    def swap(m, part, other, number):
        upper = m[0:32, :] - m[64:96, :]
        lower = m[32:64, :] - m[96:128, :]
        part[...] = jnp.where(core == 0, lower, upper)
        transfer = pltpu.make_async_remote_copy(
            src_ref=part, dst_ref=other, send_sem=pair_send.at[number], recv_sem=pair_recv.at[number],
            device_id={"c": 1 - core}, device_id_type=MESH,
        )
        transfer.start()
        return jnp.where(core == 0, upper, lower), transfer

    kept, pair = swap(mq, part_q, other_q, 0)

    gather_q = Gather(all_q, 40, place, core, "x", "y", (a_send, a_recv, a_die_send, a_die_recv))
    gather_k = Gather(all_k, 32, place, core, "y", "x", (b_send, b_recv, b_die_send, b_die_recv))
    mk[...] = jnp.zeros_like(mk)
    carry[...] = jnp.zeros_like(carry)
    for group in range(4):
        key_backward(group, kbuf, vext, slope, carry, diag, back, mk)
    kept_k, pair_k = swap(mk, part_k, other_k, 1)
    pair.wait_recv()
    q_first = pl.multiple_of(gather_q.first_row(core, y, x), 8)
    all_q[pl.ds(q_first, 32), :] = kept + other_q[...]
    total = energy[...]
    for dz in range(1, 8):
        z_copies[dz - 1].wait_recv()
        total = total + energies[dz]
    all_q[pl.ds(q_first + 32, 8), :] = total
    gather_q.start()
    pair_k.wait_recv()
    all_k[pl.ds(pl.multiple_of(gather_k.first_row(core, x, y), 8), 32), :] = kept_k + other_k[...]
    gather_k.start()
    gather_q.second()
    gather_k.second()
    for i in range(3):
        gather_q.third(i)
        gather_k.third(i)
    for i in range(4):
        gather_q.wait_handed(i)
    tiles = [all_q[d * 40 + 32 : d * 40 + 40, :] for d in range(32)]
    while len(tiles) > 1:
        tiles = [p + q for p, q in zip(tiles[0::2], tiles[1::2])]
    sums = jnp.sum(jnp.sum(tiles[0], axis=0, keepdims=True), axis=1, keepdims=True)
    inverse = 1.0 / sums
    for i in range(4):
        gather_k.wait_handed(i)
    for c in range(2):
        for head in range(16):
            at_q = (c * 16 + (head % 4) * 4 + head // 4) * 40
            at_k = (c * 16 + head) * 32
            out_q[head, c * 32 : c * 32 + 32, :] = all_q[at_q : at_q + 32, :] * inverse
            out_k[head, c * 32 : c * 32 + 32, :] = all_k[at_k : at_k + 32, :] * inverse

    @pl.when(target_core != core)
    def _():
        q_copy(0).wait_send()

    for r in range(1, 16):
        q_copy(r).wait_send()
    for c in z_copies + [pair, pair_k]:
        c.wait_send()
    for g in (gather_keys, gather_values, gather_q, gather_k):
        g.wait_sent()


Q_EARLY = 15
V_EARLY = True


def feature_parts(logit):
    slope = jnp.exp(jnp.minimum(logit, 0.0))
    return slope + jnp.maximum(logit, 0.0), slope


def signed(w_ref):
    hi, lo = split(jnp.concatenate([w_ref[...], -w_ref[...]], axis=0))
    return jnp.concatenate([hi, lo], axis=1)


def key_features(at_y, wk2, kin, kbuf, phi_hi, phi_lo, slope):
    for at_x in range(4):
        j = at_x * 4 + at_y
        keys = jnp.concatenate(
            [kin[rows((c * 16 + at_y * 4 + at_x) * 128, 128), :] for c in range(2)], axis=0
        )
        kbuf[rows(j * 256, 256), :] = keys
        phi, s = feature_parts(nt(wk2, jnp.concatenate([keys, keys], axis=1)))
        slope[j] = s
        phi_hi[j], phi_lo[j] = split(phi)


def states(vext, phi_hi, phi_lo, carry, state_hi, state_lo):
    carry[...] = jnp.zeros_like(carry)

    @pl.loop(0, 4)
    def _(group):
        before = carry[...]
        for i in range(4):
            j = group * 4 + i
            state_hi[j], state_lo[j] = split(before)
            both = nn(
                jnp.concatenate([phi_hi[j], phi_lo[j]], axis=0), vext[rows(j * 256, 256), :]
            )
            before = before + (both[0:128] + both[128:256])
        carry[...] = before


def first_scores(core, pair):
    return jnp.where(core == 0, (0, 1, 3, 10)[pair], (0, 3, 7, 12)[pair])


def teacher_scores(pair, core, qbuf, kbuf, scores, peak):
    scale = math.log2(math.e) / math.sqrt(128.0)
    base = first_scores(core, pair)
    last = chunk_of(core, 2 * pair) // 2
    q = qbuf[pl.ds(pair * 512, 512), :]

    def widest(s, top):
        for i in range(4):
            top = jnp.maximum(top, s[:, i * 128 : (i + 1) * 128])
        return top

    s = nt(q, kbuf[rows(last * 512, 512), :]) * scale
    row = lax.broadcasted_iota(jnp.int32, (512, 512), 0)
    col = lax.broadcasted_iota(jnp.int32, (512, 512), 1)
    s = jnp.where(col <= row, s, -1e30)
    scores[base + last] = s
    peak[pair] = widest(s, jnp.full((512, 128), -1e30, F32))

    @pl.loop(0, last)
    def _(jj):
        s = nt(q, kbuf[rows(jj * 512, 512), :]) * scale
        scores[base + jj] = s
        peak[pair] = widest(s, peak[pair])

    peak[pair] = jnp.broadcast_to(jnp.max(peak[pair], axis=1, keepdims=True), (512, 128))


def teacher_weights(pair, core, vext, scores, peak, acc, teacher_out, energy):
    base = first_scores(core, pair)
    last = chunk_of(core, 2 * pair) // 2
    acc[...] = jnp.zeros_like(acc)

    @pl.loop(0, last + 1)
    def _(jj):
        for i in range(2):
            top = peak[pair]
            w = [
                jnp.exp2(scores[base + jj, :, (2 * i + h) * 128 : (2 * i + h + 1) * 128] - top)
                for h in range(2)
            ]
            w = jnp.concatenate(w, axis=1).astype(BF16)
            acc[...] += nn(w, vext[rows(jj * 512 + i * 256, 256), :])

    t = acc[:, 0:128] / acc[:, 128:256]
    teacher_out[2 * pair] = t[0:256]
    teacher_out[2 * pair + 1] = t[256:512]
    energy[...] += jnp.sum((t * t).reshape(64, 8, 128), axis=0)


def student(
    core, qbuf, vext, wq_t, teacher_out, phi_hi, phi_lo, state_hi, state_lo, diag, back, mq
):
    wq2 = signed(wq_t)
    mq[...] = jnp.zeros_like(mq)
    row = lax.broadcasted_iota(jnp.int32, (256, 256), 0)
    col = lax.broadcasted_iota(jnp.int32, (256, 256), 1)
    visible = col <= row

    def one(slot):
        chunk = chunk_of(core, slot)
        q = qbuf[rows(slot * 256, 256), :]
        values = vext[rows(chunk * 256, 256), :]
        q2 = jnp.concatenate([q, q], axis=1)
        phi, _ = feature_parts(nt(q2, wq2))
        phi_t, slope_t = feature_parts(nt(wq2, q2))
        qh, ql = split(phi)
        qth, qtl = split(phi_t)
        qhh = jnp.concatenate([qh, qh], axis=1)
        qts = jnp.concatenate([qth, qtl], axis=0)
        kh, kl = phi_hi[chunk], phi_lo[chunk]
        sh, sl = state_hi[chunk], state_lo[chunk]
        ks = jnp.concatenate([kh, kl], axis=0)
        ss = jnp.concatenate([sh, sl], axis=0)
        inner = jnp.where(visible, nn(qhh, ks) + nn(ql, kh), 0.0)
        ih, il = split(inner)
        both = (nn(ih, values) + nn(il, values)) + (nn(qhh, ss) + nn(ql, sh))
        inverse = 1.0 / both[:, 128:256]
        student = both[:, 0:128] * inverse
        grad_out = LOSS_SCALE * (student - teacher_out[slot])
        grad_numer = grad_out * inverse
        gh, gl = split(jnp.concatenate([grad_numer, -(grad_numer * student)], axis=1))
        grad_inner = jnp.where(visible, nt(gh, values) + nt(gl, values), 0.0)
        gih, gil = split(grad_inner)
        back_both = nn(qts, gh)
        back[chunk] = (back_both[0:128] + back_both[128:256]) + nn(qth, gl)
        diag_both = nn(qts, gih)
        diag[chunk] = (diag_both[0:128] + diag_both[128:256]) + nn(qth, gil)
        grad_both = nt(ks, gih) + nt(ss, gh)
        grad_phi = (grad_both[0:128] + grad_both[128:256]) + (nt(kh, gil) + nt(sh, gl))
        dh, dl = split(grad_phi * slope_t)
        m_both = nn(jnp.concatenate([dh, dl], axis=0), q)
        return m_both[0:128] + m_both[128:256]

    @pl.loop(0, 8 // STUDENT_UNROLL)
    def _(step):
        parts = [one(step * STUDENT_UNROLL + h) for h in range(STUDENT_UNROLL)]
        mq[...] += sum(parts[1:], parts[0])


STUDENT_UNROLL = 2


def key_backward(group, kbuf, vext, slope, carry, diag, back, mk):
    later = carry[...]
    total = mk[...]
    for i in range(4):
        j = 15 - (group * 4 + i)
        keys = kbuf[rows(j * 256, 256), :]
        values = vext[rows(j * 256, 256), :]
        lh, ll = split(later)
        g_both = nt(jnp.concatenate([lh, ll], axis=0), values)
        grad_phi = (g_both[0:128] + g_both[128:256]) + diag[j]
        dh, dl = split(grad_phi * slope[j])
        m_both = nn(jnp.concatenate([dh, dl], axis=0), keys)
        total = total + (m_both[0:128] + m_both[128:256])
        later = later + back[j]
    mk[...] = total
    carry[...] = later


def scratch():
    v = pltpu.VMEM
    return [
        v((2048, 128), BF16), v((2048, 128), F32), v((16, 128, 128), BF16),
        v((2048, 128), BF16), v((4096, 128), BF16), v((4096, 128), BF16), v((4096, 256), BF16),
        v((4096, 128), BF16),
        v((64, 128), F32), v((64, 128), F32), v((18, 512, 512), F32), v((512, 256), F32),
        v((4, 512, 128), F32), v((8, 256, 128), F32),
        v((16, 128, 256), BF16), v((16, 128, 256), BF16), v((16, 128, 256), F32),
        v((16, 128, 256), BF16), v((16, 128, 256), BF16), v((128, 256), F32),
        v((16, 128, 256), F32), v((16, 128, 256), F32), v((128, 128), F32), v((128, 128), F32),
        v((8, 128), F32),
    ]


def exchange_scratch():
    v, dma = pltpu.VMEM, pltpu.SemaphoreType.DMA
    return [
        v((32, 128), F32), v((32, 128), F32), v((32, 128), F32), v((32, 128), F32),
        v((8, 8, 128), F32), v((32 * 40, 128), F32), v((32 * 32, 128), F32),
        dma((16,)), dma((16,)), dma((6,)),
    ] + [dma((6,)), dma((6,)), dma((4,)), dma((4,))] * 4 + [dma((2,)), dma((2,)), dma((8,)), dma((8,))]


def on_device(queries, key_states, value_vector_states, map_query, map_key):
    far = pl.BlockSpec(memory_space=pltpu.HBM)
    whole = pl.BlockSpec(memory_space=pltpu.VMEM)
    grad_query, grad_key = pl.pallas_call(
        kernel,
        out_shape=(jax.ShapeDtypeStruct((16, 64, 128), F32),) * 2,
        in_specs=[far] * 5,
        out_specs=(whole, whole),
        scratch_shapes=scratch() + exchange_scratch(),
        compiler_params=pltpu.CompilerParams(
            collective_id=0, has_side_effects=True, vmem_limit_bytes=60 * 1024 * 1024
        ),
        name="transfer_step",
    )(
        queries.reshape(2048, 128),
        key_states.reshape(128, 128),
        value_vector_states.reshape(128, 128),
        jnp.swapaxes(map_query, 1, 2),
        jnp.swapaxes(map_key, 1, 2),
    )
    return jnp.swapaxes(grad_query, 1, 2), jnp.swapaxes(grad_key, 1, 2)


def solution(mesh):
    torus = Mesh(mesh.devices.reshape(4, 4, 2, mesh.shape["head"]), ("x", "y", "c", "z"))
    ctx = ("x", "y", "c")
    in_specs = (
        P(ctx, "z", None),
        P(ctx, "z", None),
        P(ctx, "z", None),
        P("z", None, None),
        P("z", None, None),
    )
    out_specs = (P("z", None, None), P("z", None, None))
    return jax.shard_map(
        on_device, mesh=torus, in_specs=in_specs, out_specs=out_specs, check_vma=False
    )
```

```python
import math

import jax
import jax.numpy as jnp
from jax import lax
from jax.experimental import pallas as pl
from jax.experimental.pallas import tpu as pltpu
from jax.sharding import Mesh
from jax.sharding import PartitionSpec as P

F32 = jnp.float32
BF16 = jnp.bfloat16
MESH = pl.DeviceIdType.MESH
HALF = 64
LOSS_SCALE = 256.0


def nn(a, b):
    return lax.dot_general(a, b, (((1,), (0,)), ((), ())), preferred_element_type=F32)


def nt(a, b):
    return lax.dot_general(a, b, (((1,), (1,)), ((), ())), preferred_element_type=F32)


def split(value):
    high = value.astype(BF16)
    return high, (value - high.astype(F32)).astype(BF16)


def rows(start, size):
    return pl.ds(pl.multiple_of(start, size), size)


def owner_of(chunk_x):
    return jnp.where((chunk_x == 0) | (chunk_x == 3), 0, 1)


def chunk_of(core, slot):
    return jnp.where(core == 0, jnp.where(slot < 4, slot, slot + 8), slot + 4)


class Gather:
    def __init__(self, buffer, size, place, core, a, b, sems):
        self.buffer, self.size, self.place, self.core, self.a, self.b = buffer, size, place, core, a, b
        self.send_sem, self.recv_sem, self.die_send, self.die_recv = sems
        self.sent = []

    def first_row(self, core, at_b, at_a):
        return ((core * 4 + at_b) * 4 + at_a) * self.size

    def copy(self, start, count, target, sem, send_sem, recv_sem):
        where = pl.ds(pl.multiple_of(start, 8), count * self.size)
        return pltpu.make_async_remote_copy(
            src_ref=self.buffer.at[where],
            dst_ref=self.buffer.at[where],
            send_sem=send_sem.at[sem],
            recv_sem=recv_sem.at[sem],
            device_id=target,
            device_id_type=MESH,
        )

    def send(self, *args):
        transfer = self.copy(*args)
        transfer.start()
        self.sent.append(transfer)

    def start(self):
        here_a, here_b = self.place[self.a], self.place[self.b]
        for i, off in enumerate(OFFSETS):
            self.send(
                self.first_row(self.core, here_b, here_a), 1, {self.a: lax.rem(here_a + off, 4)},
                i, self.send_sem, self.recv_sem,
            )

    def second(self):
        here_a, here_b = self.place[self.a], self.place[self.b]
        for i, off in enumerate(OFFSETS):
            self.copy(
                self.first_row(self.core, here_b, lax.rem(here_a + 4 - off, 4)), 1,
                {self.a: here_a}, i, self.send_sem, self.recv_sem,
            ).wait_recv()
        for i, off in enumerate(OFFSETS):
            self.send(
                self.first_row(self.core, here_b, 0), 4, {self.b: lax.rem(here_b + off, 4)},
                3 + i, self.send_sem, self.recv_sem,
            )
        self.hand_over(3, 0)

    def hand_over(self, i, off):
        at_b = lax.rem(self.place[self.b] + 4 - off, 4)
        self.send(
            self.first_row(self.core, at_b, 0), 4, {"c": 1 - self.core}, i, self.die_send, self.die_recv
        )

    def third(self, i):
        at_b = lax.rem(self.place[self.b] + 4 - OFFSETS[i], 4)
        self.copy(
            self.first_row(self.core, at_b, 0), 4, {self.b: at_b}, 3 + i, self.send_sem, self.recv_sem
        ).wait_recv()
        self.hand_over(i, OFFSETS[i])

    def wait_handed(self, i):
        off = OFFSETS[i] if i < 3 else 0
        at_b = lax.rem(self.place[self.b] + 4 - off, 4)
        self.copy(
            self.first_row(1 - self.core, at_b, 0), 4, {"c": 1 - self.core}, i, self.die_send, self.die_recv
        ).wait_recv()
        return at_b

    def wait_sent(self):
        for transfer in self.sent:
            transfer.wait_send()


OFFSETS = (1, 3, 2)


def kernel(
    q_hbm, k_hbm, v_hbm, wq_hbm, wk_hbm, out_q, out_k, q_raw, q_wide, q_heads,
    qbuf, kbuf, kin, vext, vbuf, wq_t, wk_t, scores, acc, peak, teacher_out,
    phi_hi, phi_lo, slope, state_hi, state_lo, carry, diag, back, mq, mk, energy,
    part_q, part_k, other_q, other_k, energies, all_q, all_k,
    q_send, q_recv, local_sem, ici_send, ici_recv, die_send, die_recv,
    v_send, v_recv, v_die_send, v_die_recv,
    a_send, a_recv, a_die_send, a_die_recv, b_send, b_recv, b_die_send, b_die_recv,
    pair_send, pair_recv, z_send, z_recv,
):
    x, y, core, z = (lax.axis_index(n) for n in ("x", "y", "c", "z"))
    chip = x * 4 + y
    place = {"x": x, "y": y}

    local = [
        pltpu.make_async_copy(k_hbm, kin.at[rows((core * 16 + y * 4 + x) * 128, 128)], local_sem.at[0]),
        pltpu.make_async_copy(v_hbm, vbuf.at[rows((core * 16 + chip) * 128, 128)], local_sem.at[1]),
        pltpu.make_async_copy(wq_hbm.at[chip], wq_t, local_sem.at[2]),
        pltpu.make_async_copy(wk_hbm.at[chip], wk_t, local_sem.at[3]),
        pltpu.make_async_copy(q_hbm, q_raw, local_sem.at[5]),
    ]
    for c in local:
        c.start()
    barrier = pltpu.get_barrier_semaphore()
    peers = 0
    for dx in range(4):
        for dy in range(4):
            for dc in range(2):
                if dx or dy or dc:
                    target = {"x": lax.rem(x + dx, 4), "y": lax.rem(y + dy, 4), "c": lax.rem(core + dc, 2)}
                    pl.semaphore_signal(barrier, inc=1, device_id=target, device_id_type=MESH)
                    peers += 1
    for dz in range(1, 8):
        pl.semaphore_signal(barrier, inc=1, device_id={"z": lax.rem(z + dz, 8)}, device_id_type=MESH)
        peers += 1
    vext[:, 128:256] = jnp.ones((4096, 128), BF16)
    diag[...] = jnp.zeros_like(diag)
    back[...] = jnp.zeros_like(back)
    for c in local:
        c.wait()
    q_wide[...] = q_raw[...].astype(F32)
    for head in range(16):
        q_heads[head] = q_wide[pl.ds(head, 128, stride=16), :].astype(BF16)
    pl.semaphore_wait(barrier, peers)

    target_core = owner_of(x)
    my_slot = jnp.where(x >= 2, 4, 0) + y
    q_rows = rows((my_slot * 2 + core) * 128, 128)
    q_index = my_slot * 2 + core

    def q_copy(r):
        head = lax.rem(chip + r, 16)
        return pltpu.make_async_remote_copy(
            src_ref=q_heads.at[head],
            dst_ref=qbuf.at[q_rows],
            send_sem=q_send.at[r],
            recv_sem=q_recv.at[q_index],
            device_id={"x": head // 4, "y": lax.rem(head, 4), "c": target_core},
            device_id_type=MESH,
        )

    q_self = pltpu.make_async_copy(q_heads.at[chip], qbuf.at[q_rows], local_sem.at[4])

    gather_keys = Gather(
        kin, 128, place, core, "x", "y", (ici_send, ici_recv, die_send, die_recv)
    )
    gather_values = Gather(
        vbuf, 128, place, core, "y", "x", (v_send, v_recv, v_die_send, v_die_recv)
    )
    sent_queries = [0]

    def send_queries(count):
        for _ in range(count):
            sent_queries[0] += 1
            q_copy(sent_queries[0]).start()

    wk2 = signed(wk_t)
    gather_keys.start()

    @pl.when(target_core == core)
    def _():
        q_self.start()

    @pl.when(target_core != core)
    def _():
        q_copy(0).start()

    send_queries(Q_EARLY)
    if V_EARLY:
        gather_values.start()
    gather_keys.second()
    send_queries(15 - Q_EARLY)
    if not V_EARLY:
        gather_values.start()
    gather_values.second()
    for i in range(3):
        gather_keys.third(i)
    for i in (3, 0, 1, 2):
        key_features(gather_keys.wait_handed(i), wk2, kin, kbuf, phi_hi, phi_lo, slope)

    for slot in range(8):
        source = chunk_of(core, slot)
        for c in range(2):

            @pl.when((source != chip) | (core != c))
            def _(slot=slot, c=c):
                pltpu.make_async_remote_copy(
                    src_ref=q_heads.at[0],
                    dst_ref=qbuf.at[pl.ds((slot * 2 + c) * 128, 128)],
                    send_sem=q_send.at[0],
                    recv_sem=q_recv.at[slot * 2 + c],
                    device_id={"c": core},
                    device_id_type=MESH,
                ).wait_recv()

    @pl.when(target_core == core)
    def _():
        q_self.wait()

    for i in range(3):
        gather_values.third(i)
    teacher_scores(core, qbuf, kbuf, scores, peak)
    for i in (3, 0, 1, 2):
        gather_values.wait_handed(i)
    for c in range(2):
        for j in range(16):
            vext[j * 256 + c * 128 : j * 256 + c * 128 + 128, 0:128] = vbuf[
                (c * 16 + j) * 128 : (c * 16 + j + 1) * 128, :
            ]
    states(vext, phi_hi, phi_lo, carry, state_hi, state_lo)
    energy[...] = jnp.zeros_like(energy)
    teacher_weights(core, vext, scores, peak, acc, teacher_out, energy)

    z_copies = []
    for dz in range(1, 8):
        c = pltpu.make_async_remote_copy(
            src_ref=energy, dst_ref=energies.at[dz], send_sem=z_send.at[dz], recv_sem=z_recv.at[dz],
            device_id={"z": lax.rem(z + dz, 8)}, device_id_type=MESH,
        )
        c.start()
        z_copies.append(c)

    student(
        core, qbuf, vext, wq_t, teacher_out, phi_hi, phi_lo, state_hi, state_lo, diag, back, mq
    )

    def swap(m, part, other, number):
        upper = m[0:32, :] - m[64:96, :]
        lower = m[32:64, :] - m[96:128, :]
        part[...] = jnp.where(core == 0, lower, upper)
        transfer = pltpu.make_async_remote_copy(
            src_ref=part, dst_ref=other, send_sem=pair_send.at[number], recv_sem=pair_recv.at[number],
            device_id={"c": 1 - core}, device_id_type=MESH,
        )
        transfer.start()
        return jnp.where(core == 0, upper, lower), transfer

    kept, pair = swap(mq, part_q, other_q, 0)

    gather_q = Gather(all_q, 40, place, core, "x", "y", (a_send, a_recv, a_die_send, a_die_recv))
    gather_k = Gather(all_k, 32, place, core, "y", "x", (b_send, b_recv, b_die_send, b_die_recv))
    mk[...] = jnp.zeros_like(mk)
    carry[...] = jnp.zeros_like(carry)
    for group in range(4):
        key_backward(group, kbuf, vext, slope, carry, diag, back, mk)
    kept_k, pair_k = swap(mk, part_k, other_k, 1)
    pair.wait_recv()
    q_first = pl.multiple_of(gather_q.first_row(core, y, x), 8)
    all_q[pl.ds(q_first, 32), :] = kept + other_q[...]
    total = energy[...]
    for dz in range(1, 8):
        z_copies[dz - 1].wait_recv()
        total = total + energies[dz]
    all_q[pl.ds(q_first + 32, 8), :] = total
    gather_q.start()
    pair_k.wait_recv()
    all_k[pl.ds(pl.multiple_of(gather_k.first_row(core, x, y), 8), 32), :] = kept_k + other_k[...]
    gather_k.start()
    gather_q.second()
    gather_k.second()
    for i in range(3):
        gather_q.third(i)
        gather_k.third(i)
    for i in range(4):
        gather_q.wait_handed(i)
    tiles = [all_q[d * 40 + 32 : d * 40 + 40, :] for d in range(32)]
    while len(tiles) > 1:
        tiles = [p + q for p, q in zip(tiles[0::2], tiles[1::2])]
    sums = jnp.sum(jnp.sum(tiles[0], axis=0, keepdims=True), axis=1, keepdims=True)
    inverse = 1.0 / sums
    for i in range(4):
        gather_k.wait_handed(i)
    for c in range(2):
        for head in range(16):
            at_q = (c * 16 + (head % 4) * 4 + head // 4) * 40
            at_k = (c * 16 + head) * 32
            out_q[head, c * 32 : c * 32 + 32, :] = all_q[at_q : at_q + 32, :] * inverse
            out_k[head, c * 32 : c * 32 + 32, :] = all_k[at_k : at_k + 32, :] * inverse

    @pl.when(target_core != core)
    def _():
        q_copy(0).wait_send()

    for r in range(1, 16):
        q_copy(r).wait_send()
    for c in z_copies + [pair, pair_k]:
        c.wait_send()
    for g in (gather_keys, gather_values, gather_q, gather_k):
        g.wait_sent()


Q_EARLY = 15
V_EARLY = True


def feature_parts(logit):
    slope = jnp.exp(jnp.minimum(logit, 0.0))
    return slope + jnp.maximum(logit, 0.0), slope


def signed(w_ref):
    hi, lo = split(jnp.concatenate([w_ref[...], -w_ref[...]], axis=0))
    return jnp.concatenate([hi, lo], axis=1)


def key_features(at_y, wk2, kin, kbuf, phi_hi, phi_lo, slope):
    for at_x in range(4):
        j = at_x * 4 + at_y
        keys = jnp.concatenate(
            [kin[rows((c * 16 + at_y * 4 + at_x) * 128, 128), :] for c in range(2)], axis=0
        )
        kbuf[rows(j * 256, 256), :] = keys
        phi, s = feature_parts(nt(wk2, jnp.concatenate([keys, keys], axis=1)))
        slope[j] = s
        phi_hi[j], phi_lo[j] = split(phi)


def states(vext, phi_hi, phi_lo, carry, state_hi, state_lo):
    carry[...] = jnp.zeros_like(carry)

    @pl.loop(0, 4)
    def _(group):
        before = carry[...]
        for i in range(4):
            j = group * 4 + i
            state_hi[j], state_lo[j] = split(before)
            both = nn(
                jnp.concatenate([phi_hi[j], phi_lo[j]], axis=0), vext[rows(j * 256, 256), :]
            )
            before = before + (both[0:128] + both[128:256])
        carry[...] = before


def blocks_before(core, pair):
    return jnp.where(core == 0, (0, 1, 3, 10)[pair], (0, 3, 7, 12)[pair])


def pair_and_key(core, block):
    pair = sum((block >= blocks_before(core, p)).astype(jnp.int32) for p in range(1, 4))
    start = blocks_before(core, 0)
    for p in range(1, 4):
        start = jnp.where(pair == p, blocks_before(core, p), start)
    return pair, block - start


def widest(s, top):
    for i in range(4):
        top = jnp.maximum(top, s[:, i * 128 : (i + 1) * 128])
    return top


def teacher_scores(core, qbuf, kbuf, scores, peak):
    scale = math.log2(math.e) / math.sqrt(128.0)
    row = lax.broadcasted_iota(jnp.int32, (512, 512), 0)
    col = lax.broadcasted_iota(jnp.int32, (512, 512), 1)
    for pair in range(4):
        last = chunk_of(core, 2 * pair) // 2
        q = qbuf[pl.ds(pair * 512, 512), :]
        s = jnp.where(col <= row, nt(q, kbuf[rows(last * 512, 512), :]) * scale, -1e30)
        scores[blocks_before(core, pair) + last] = s
        peak[pair] = widest(s, jnp.full((512, 128), -1e30, F32))

    @pl.loop(0, 14 // SCORE_UNROLL)
    def _(step):
        for i in range(SCORE_UNROLL):
            n = step * SCORE_UNROLL + i
            pair = sum(
                (n >= blocks_before(core, p) - p).astype(jnp.int32) for p in range(1, 4)
            )
            block = n + pair
            _, jj = pair_and_key(core, block)
            s = nt(qbuf[rows(pair * 512, 512), :], kbuf[rows(jj * 512, 512), :]) * scale
            scores[block] = s
            peak[pair] = widest(s, peak[pair])

    for pair in range(4):
        peak[pair] = jnp.broadcast_to(jnp.max(peak[pair], axis=1, keepdims=True), (512, 128))


def teacher_weights(core, vext, scores, peak, acc, teacher_out, energy):
    acc[...] = jnp.zeros_like(acc)

    @pl.loop(0, 18 // WEIGHT_UNROLL)
    def _(step):
        for i in range(WEIGHT_UNROLL):
            block = step * WEIGHT_UNROLL + i
            pair, jj = pair_and_key(core, block)
            top = peak[pair]
            total = None
            for h in range(2):
                w = [
                    jnp.exp2(scores[block, :, (2 * h + g) * 128 : (2 * h + g + 1) * 128] - top)
                    for g in range(2)
                ]
                w = jnp.concatenate(w, axis=1).astype(BF16)
                part = nn(w, vext[rows(jj * 512 + h * 256, 256), :])
                total = part if total is None else total + part
            acc[pair] += total

    for pair in range(4):
        t = acc[pair, :, 0:128] / acc[pair, :, 128:256]
        teacher_out[2 * pair] = t[0:256]
        teacher_out[2 * pair + 1] = t[256:512]
        energy[...] += jnp.sum((t * t).reshape(64, 8, 128), axis=0)


SCORE_UNROLL = 7
WEIGHT_UNROLL = 3


def student(
    core, qbuf, vext, wq_t, teacher_out, phi_hi, phi_lo, state_hi, state_lo, diag, back, mq
):
    wq2 = signed(wq_t)
    mq[...] = jnp.zeros_like(mq)
    row = lax.broadcasted_iota(jnp.int32, (256, 256), 0)
    col = lax.broadcasted_iota(jnp.int32, (256, 256), 1)
    visible = col <= row

    def one(slot):
        chunk = chunk_of(core, slot)
        q = qbuf[rows(slot * 256, 256), :]
        values = vext[rows(chunk * 256, 256), :]
        q2 = jnp.concatenate([q, q], axis=1)
        phi, _ = feature_parts(nt(q2, wq2))
        phi_t, slope_t = feature_parts(nt(wq2, q2))
        qh, ql = split(phi)
        qth, qtl = split(phi_t)
        qhh = jnp.concatenate([qh, qh], axis=1)
        qts = jnp.concatenate([qth, qtl], axis=0)
        kh, kl = phi_hi[chunk], phi_lo[chunk]
        sh, sl = state_hi[chunk], state_lo[chunk]
        ks = jnp.concatenate([kh, kl], axis=0)
        ss = jnp.concatenate([sh, sl], axis=0)
        inner = jnp.where(visible, nn(qhh, ks) + nn(ql, kh), 0.0)
        ih, il = split(inner)
        both = (nn(ih, values) + nn(il, values)) + (nn(qhh, ss) + nn(ql, sh))
        inverse = 1.0 / both[:, 128:256]
        student = both[:, 0:128] * inverse
        grad_out = LOSS_SCALE * (student - teacher_out[slot])
        grad_numer = grad_out * inverse
        gh, gl = split(jnp.concatenate([grad_numer, -(grad_numer * student)], axis=1))
        grad_inner = jnp.where(visible, nt(gh, values) + nt(gl, values), 0.0)
        gih, gil = split(grad_inner)
        back_both = nn(qts, gh)
        back[chunk] = (back_both[0:128] + back_both[128:256]) + nn(qth, gl)
        diag_both = nn(qts, gih)
        diag[chunk] = (diag_both[0:128] + diag_both[128:256]) + nn(qth, gil)
        grad_both = nt(ks, gih) + nt(ss, gh)
        grad_phi = (grad_both[0:128] + grad_both[128:256]) + (nt(kh, gil) + nt(sh, gl))
        dh, dl = split(grad_phi * slope_t)
        m_both = nn(jnp.concatenate([dh, dl], axis=0), q)
        return m_both[0:128] + m_both[128:256]

    @pl.loop(0, 8 // STUDENT_UNROLL)
    def _(step):
        parts = [one(step * STUDENT_UNROLL + h) for h in range(STUDENT_UNROLL)]
        mq[...] += sum(parts[1:], parts[0])


STUDENT_UNROLL = 4


def key_backward(group, kbuf, vext, slope, carry, diag, back, mk):
    later = carry[...]
    total = mk[...]
    for i in range(4):
        j = 15 - (group * 4 + i)
        keys = kbuf[rows(j * 256, 256), :]
        values = vext[rows(j * 256, 256), :]
        lh, ll = split(later)
        g_both = nt(jnp.concatenate([lh, ll], axis=0), values)
        grad_phi = (g_both[0:128] + g_both[128:256]) + diag[j]
        dh, dl = split(grad_phi * slope[j])
        m_both = nn(jnp.concatenate([dh, dl], axis=0), keys)
        total = total + (m_both[0:128] + m_both[128:256])
        later = later + back[j]
    mk[...] = total
    carry[...] = later


def scratch():
    v = pltpu.VMEM
    return [
        v((2048, 128), BF16), v((2048, 128), F32), v((16, 128, 128), BF16),
        v((2048, 128), BF16), v((4096, 128), BF16), v((4096, 128), BF16), v((4096, 256), BF16),
        v((4096, 128), BF16),
        v((64, 128), F32), v((64, 128), F32), v((18, 512, 512), F32), v((4, 512, 256), F32),
        v((4, 512, 128), F32), v((8, 256, 128), F32),
        v((16, 128, 256), BF16), v((16, 128, 256), BF16), v((16, 128, 256), F32),
        v((16, 128, 256), BF16), v((16, 128, 256), BF16), v((128, 256), F32),
        v((16, 128, 256), F32), v((16, 128, 256), F32), v((128, 128), F32), v((128, 128), F32),
        v((8, 128), F32),
    ]


def exchange_scratch():
    v, dma = pltpu.VMEM, pltpu.SemaphoreType.DMA
    return [
        v((32, 128), F32), v((32, 128), F32), v((32, 128), F32), v((32, 128), F32),
        v((8, 8, 128), F32), v((32 * 40, 128), F32), v((32 * 32, 128), F32),
        dma((16,)), dma((16,)), dma((6,)),
    ] + [dma((6,)), dma((6,)), dma((4,)), dma((4,))] * 4 + [dma((2,)), dma((2,)), dma((8,)), dma((8,))]


def on_device(queries, key_states, value_vector_states, map_query, map_key):
    far = pl.BlockSpec(memory_space=pltpu.HBM)
    whole = pl.BlockSpec(memory_space=pltpu.VMEM)
    grad_query, grad_key = pl.pallas_call(
        kernel,
        out_shape=(jax.ShapeDtypeStruct((16, 64, 128), F32),) * 2,
        in_specs=[far] * 5,
        out_specs=(whole, whole),
        scratch_shapes=scratch() + exchange_scratch(),
        compiler_params=pltpu.CompilerParams(
            collective_id=0, has_side_effects=True, vmem_limit_bytes=50 * 1024 * 1024
        ),
        name="transfer_step",
    )(
        *(
            pltpu.with_memory_space_constraint(operand, pltpu.HBM)
            for operand in (
                queries.reshape(2048, 128),
                key_states.reshape(128, 128),
                value_vector_states.reshape(128, 128),
                jnp.swapaxes(map_query, 1, 2),
                jnp.swapaxes(map_key, 1, 2),
            )
        ),
    )
    return jnp.swapaxes(grad_query, 1, 2), jnp.swapaxes(grad_key, 1, 2)


def solution(mesh):
    torus = Mesh(mesh.devices.reshape(4, 4, 2, mesh.shape["head"]), ("x", "y", "c", "z"))
    ctx = ("x", "y", "c")
    in_specs = (
        P(ctx, "z", None),
        P(ctx, "z", None),
        P(ctx, "z", None),
        P("z", None, None),
        P("z", None, None),
    )
    out_specs = (P("z", None, None), P("z", None, None))
    return jax.shard_map(
        on_device, mesh=torus, in_specs=in_specs, out_specs=out_specs, check_vma=False
    )
```

```python
import math

import jax
import jax.numpy as jnp
from jax import lax
from jax.experimental import pallas as pl
from jax.experimental.pallas import tpu as pltpu
from jax.sharding import Mesh
from jax.sharding import PartitionSpec as P

F32 = jnp.float32
BF16 = jnp.bfloat16
MESH = pl.DeviceIdType.MESH
HALF = 64
LOSS_SCALE = 256.0


def nn(a, b):
    return lax.dot_general(a, b, (((1,), (0,)), ((), ())), preferred_element_type=F32)


def nt(a, b):
    return lax.dot_general(a, b, (((1,), (1,)), ((), ())), preferred_element_type=F32)


def split(value):
    high = value.astype(BF16)
    return high, (value - high.astype(F32)).astype(BF16)


def rows(start, size):
    return pl.ds(pl.multiple_of(start, size), size)


def owner_of(chunk_x):
    return jnp.where((chunk_x == 0) | (chunk_x == 3), 0, 1)


def chunk_of(core, slot):
    return jnp.where(core == 0, jnp.where(slot < 4, slot, slot + 8), slot + 4)


class Gather:
    def __init__(self, buffer, size, place, core, a, b, sems):
        self.buffer, self.size, self.place, self.core, self.a, self.b = buffer, size, place, core, a, b
        self.send_sem, self.recv_sem, self.die_send, self.die_recv = sems
        self.sent = []

    def first_row(self, core, at_b, at_a):
        return ((core * 4 + at_b) * 4 + at_a) * self.size

    def copy(self, start, count, target, sem, send_sem, recv_sem):
        where = pl.ds(pl.multiple_of(start, 8), count * self.size)
        return pltpu.make_async_remote_copy(
            src_ref=self.buffer.at[where],
            dst_ref=self.buffer.at[where],
            send_sem=send_sem.at[sem],
            recv_sem=recv_sem.at[sem],
            device_id=target,
            device_id_type=MESH,
        )

    def send(self, *args):
        transfer = self.copy(*args)
        transfer.start()
        self.sent.append(transfer)

    def start(self):
        here_a, here_b = self.place[self.a], self.place[self.b]
        for i, off in enumerate(OFFSETS):
            self.send(
                self.first_row(self.core, here_b, here_a), 1, {self.a: lax.rem(here_a + off, 4)},
                i, self.send_sem, self.recv_sem,
            )

    def second(self):
        here_a, here_b = self.place[self.a], self.place[self.b]
        for i, off in enumerate(OFFSETS):
            self.copy(
                self.first_row(self.core, here_b, lax.rem(here_a + 4 - off, 4)), 1,
                {self.a: here_a}, i, self.send_sem, self.recv_sem,
            ).wait_recv()
        for i, off in enumerate(OFFSETS):
            self.send(
                self.first_row(self.core, here_b, 0), 4, {self.b: lax.rem(here_b + off, 4)},
                3 + i, self.send_sem, self.recv_sem,
            )
        self.hand_over(3, 0)

    def hand_over(self, i, off):
        at_b = lax.rem(self.place[self.b] + 4 - off, 4)
        self.send(
            self.first_row(self.core, at_b, 0), 4, {"c": 1 - self.core}, i, self.die_send, self.die_recv
        )

    def third(self, i):
        at_b = lax.rem(self.place[self.b] + 4 - OFFSETS[i], 4)
        self.copy(
            self.first_row(self.core, at_b, 0), 4, {self.b: at_b}, 3 + i, self.send_sem, self.recv_sem
        ).wait_recv()
        self.hand_over(i, OFFSETS[i])

    def wait_handed(self, i):
        off = OFFSETS[i] if i < 3 else 0
        at_b = lax.rem(self.place[self.b] + 4 - off, 4)
        self.copy(
            self.first_row(1 - self.core, at_b, 0), 4, {"c": 1 - self.core}, i, self.die_send, self.die_recv
        ).wait_recv()
        return at_b

    def wait_sent(self):
        for transfer in self.sent:
            transfer.wait_send()


OFFSETS = (1, 3, 2)


def kernel(
    q_hbm, k_hbm, v_hbm, wq_hbm, wk_hbm, out_q, out_k, q_raw, q_wide, q_heads,
    qbuf, kbuf, kin, vext, vbuf, wq_t, wk_t, scores, acc, peak, teacher_out,
    phi_hi, phi_lo, slope, state_hi, state_lo, carry, diag, back, mq, mk, energy,
    part_q, part_k, other_q, other_k, energies, all_q, all_k,
    q_send, q_recv, local_sem, ici_send, ici_recv, die_send, die_recv,
    v_send, v_recv, v_die_send, v_die_recv,
    a_send, a_recv, a_die_send, a_die_recv, b_send, b_recv, b_die_send, b_die_recv,
    pair_send, pair_recv, z_send, z_recv,
):
    x, y, core, z = (lax.axis_index(n) for n in ("x", "y", "c", "z"))
    chip = x * 4 + y
    place = {"x": x, "y": y}

    barrier = pltpu.get_barrier_semaphore()
    peers = 0
    for dz in range(1, 8):
        pl.semaphore_signal(barrier, inc=1, device_id={"z": lax.rem(z + dz, 8)}, device_id_type=MESH)
        peers += 1
    for dx in range(4):
        for dy in range(4):
            for dc in range(2):
                if dx or dy or dc:
                    target = {"x": lax.rem(x + dx, 4), "y": lax.rem(y + dy, 4), "c": lax.rem(core + dc, 2)}
                    pl.semaphore_signal(barrier, inc=1, device_id=target, device_id_type=MESH)
                    peers += 1
    local = [
        pltpu.make_async_copy(k_hbm, kin.at[rows((core * 16 + y * 4 + x) * 128, 128)], local_sem.at[0]),
        pltpu.make_async_copy(v_hbm, vbuf.at[rows((core * 16 + chip) * 128, 128)], local_sem.at[1]),
        pltpu.make_async_copy(wq_hbm.at[chip], wq_t, local_sem.at[2]),
        pltpu.make_async_copy(wk_hbm.at[chip], wk_t, local_sem.at[3]),
        pltpu.make_async_copy(q_hbm, q_raw, local_sem.at[5]),
    ]
    for c in local:
        c.start()
    vext[:, 128:256] = jnp.ones((4096, 128), BF16)
    diag[...] = jnp.zeros_like(diag)
    back[...] = jnp.zeros_like(back)
    for c in local:
        c.wait()
    q_wide[...] = q_raw[...].astype(F32)
    for head in range(16):
        q_heads[head] = q_wide[pl.ds(head, 128, stride=16), :].astype(BF16)
    pl.semaphore_wait(barrier, peers)

    target_core = owner_of(x)
    my_slot = jnp.where(x >= 2, 4, 0) + y
    q_rows = rows((my_slot * 2 + core) * 128, 128)
    q_index = my_slot * 2 + core

    def q_copy(r):
        head = lax.rem(chip + r, 16)
        return pltpu.make_async_remote_copy(
            src_ref=q_heads.at[head],
            dst_ref=qbuf.at[q_rows],
            send_sem=q_send.at[r],
            recv_sem=q_recv.at[q_index],
            device_id={"x": head // 4, "y": lax.rem(head, 4), "c": target_core},
            device_id_type=MESH,
        )

    q_self = pltpu.make_async_copy(q_heads.at[chip], qbuf.at[q_rows], local_sem.at[4])

    gather_keys = Gather(
        kin, 128, place, core, "x", "y", (ici_send, ici_recv, die_send, die_recv)
    )
    gather_values = Gather(
        vbuf, 128, place, core, "y", "x", (v_send, v_recv, v_die_send, v_die_recv)
    )
    sent_queries = [0]

    def send_queries(count):
        for _ in range(count):
            sent_queries[0] += 1
            q_copy(sent_queries[0]).start()

    wk2 = signed(wk_t)
    gather_keys.start()

    @pl.when(target_core == core)
    def _():
        q_self.start()

    @pl.when(target_core != core)
    def _():
        q_copy(0).start()

    send_queries(Q_EARLY)
    if V_EARLY:
        gather_values.start()
    gather_keys.second()
    send_queries(15 - Q_EARLY)
    if not V_EARLY:
        gather_values.start()
    gather_values.second()
    for i in range(3):
        gather_keys.third(i)
    for i in (3, 0, 1, 2):
        key_features(gather_keys.wait_handed(i), wk2, kin, kbuf, phi_hi, phi_lo, slope)

    for slot in range(8):
        source = chunk_of(core, slot)
        for c in range(2):

            @pl.when((source != chip) | (core != c))
            def _(slot=slot, c=c):
                pltpu.make_async_remote_copy(
                    src_ref=q_heads.at[0],
                    dst_ref=qbuf.at[pl.ds((slot * 2 + c) * 128, 128)],
                    send_sem=q_send.at[0],
                    recv_sem=q_recv.at[slot * 2 + c],
                    device_id={"c": core},
                    device_id_type=MESH,
                ).wait_recv()

    @pl.when(target_core == core)
    def _():
        q_self.wait()

    def hand_over_values(moment):
        for i in VALUE_STEPS[moment]:
            gather_values.third(i)

    teacher_scores(core, qbuf, kbuf, scores, peak, hand_over_values)
    for i in (3, 0, 1, 2):
        gather_values.wait_handed(i)
    for c in range(2):
        for j in range(16):
            vext[j * 256 + c * 128 : j * 256 + c * 128 + 128, 0:128] = vbuf[
                (c * 16 + j) * 128 : (c * 16 + j + 1) * 128, :
            ]
    states(vext, phi_hi, phi_lo, carry, state_hi, state_lo)
    energy[...] = jnp.zeros_like(energy)
    teacher_weights(core, vext, scores, peak, acc, teacher_out, energy)

    z_copies = []
    for dz in range(1, 8):
        c = pltpu.make_async_remote_copy(
            src_ref=energy, dst_ref=energies.at[dz], send_sem=z_send.at[dz], recv_sem=z_recv.at[dz],
            device_id={"z": lax.rem(z + dz, 8)}, device_id_type=MESH,
        )
        c.start()
        z_copies.append(c)

    student(
        core, qbuf, vext, wq_t, teacher_out, phi_hi, phi_lo, state_hi, state_lo, diag, back, mq
    )

    def swap(m, part, other, number):
        upper = m[0:32, :] - m[64:96, :]
        lower = m[32:64, :] - m[96:128, :]
        part[...] = jnp.where(core == 0, lower, upper)
        transfer = pltpu.make_async_remote_copy(
            src_ref=part, dst_ref=other, send_sem=pair_send.at[number], recv_sem=pair_recv.at[number],
            device_id={"c": 1 - core}, device_id_type=MESH,
        )
        transfer.start()
        return jnp.where(core == 0, upper, lower), transfer

    kept, pair = swap(mq, part_q, other_q, 0)

    gather_q = Gather(all_q, 40, place, core, "x", "y", (a_send, a_recv, a_die_send, a_die_recv))
    gather_k = Gather(all_k, 32, place, core, "y", "x", (b_send, b_recv, b_die_send, b_die_recv))
    mk[...] = jnp.zeros_like(mk)
    carry[...] = jnp.zeros_like(carry)
    for group in range(4):
        key_backward(group, kbuf, vext, slope, carry, diag, back, mk)
    kept_k, pair_k = swap(mk, part_k, other_k, 1)
    pair.wait_recv()
    q_first = pl.multiple_of(gather_q.first_row(core, y, x), 8)
    all_q[pl.ds(q_first, 32), :] = kept + other_q[...]
    total = energy[...]
    for dz in range(1, 8):
        z_copies[dz - 1].wait_recv()
        total = total + energies[dz]
    all_q[pl.ds(q_first + 32, 8), :] = total
    gather_q.start()
    pair_k.wait_recv()
    all_k[pl.ds(pl.multiple_of(gather_k.first_row(core, x, y), 8), 32), :] = kept_k + other_k[...]
    gather_k.start()
    gather_q.second()
    gather_k.second()
    for i in range(3):
        gather_q.third(i)
        gather_k.third(i)
    for i in range(4):
        gather_q.wait_handed(i)
    tiles = [all_q[d * 40 + 32 : d * 40 + 40, :] for d in range(32)]
    while len(tiles) > 1:
        tiles = [p + q for p, q in zip(tiles[0::2], tiles[1::2])]
    sums = jnp.sum(jnp.sum(tiles[0], axis=0, keepdims=True), axis=1, keepdims=True)
    inverse = 1.0 / sums
    for i in range(4):
        gather_k.wait_handed(i)
    for c in range(2):
        for head in range(16):
            at_q = (c * 16 + (head % 4) * 4 + head // 4) * 40
            at_k = (c * 16 + head) * 32
            out_q[head, c * 32 : c * 32 + 32, :] = all_q[at_q : at_q + 32, :] * inverse
            out_k[head, c * 32 : c * 32 + 32, :] = all_k[at_k : at_k + 32, :] * inverse

    @pl.when(target_core != core)
    def _():
        q_copy(0).wait_send()

    for r in range(1, 16):
        q_copy(r).wait_send()
    for c in z_copies + [pair, pair_k]:
        c.wait_send()
    for g in (gather_keys, gather_values, gather_q, gather_k):
        g.wait_sent()


Q_EARLY = 15
V_EARLY = True


def feature_parts(logit):
    slope = jnp.exp(jnp.minimum(logit, 0.0))
    return slope + jnp.maximum(logit, 0.0), slope


def signed(w_ref):
    hi, lo = split(jnp.concatenate([w_ref[...], -w_ref[...]], axis=0))
    return jnp.concatenate([hi, lo], axis=1)


def key_features(at_y, wk2, kin, kbuf, phi_hi, phi_lo, slope):
    for at_x in range(4):
        j = at_x * 4 + at_y
        keys = jnp.concatenate(
            [kin[rows((c * 16 + at_y * 4 + at_x) * 128, 128), :] for c in range(2)], axis=0
        )
        kbuf[rows(j * 256, 256), :] = keys
        phi, s = feature_parts(nt(wk2, jnp.concatenate([keys, keys], axis=1)))
        slope[j] = s
        phi_hi[j], phi_lo[j] = split(phi)


def states(vext, phi_hi, phi_lo, carry, state_hi, state_lo):
    carry[...] = jnp.zeros_like(carry)

    @pl.loop(0, 4)
    def _(group):
        before = carry[...]
        for i in range(4):
            j = group * 4 + i
            state_hi[j], state_lo[j] = split(before)
            both = nn(
                jnp.concatenate([phi_hi[j], phi_lo[j]], axis=0), vext[rows(j * 256, 256), :]
            )
            before = before + (both[0:128] + both[128:256])
        carry[...] = before


def blocks_before(core, pair):
    return jnp.where(core == 0, (0, 1, 3, 10)[pair], (0, 3, 7, 12)[pair])


def pair_and_key(core, block):
    pair = sum((block >= blocks_before(core, p)).astype(jnp.int32) for p in range(1, 4))
    start = blocks_before(core, 0)
    for p in range(1, 4):
        start = jnp.where(pair == p, blocks_before(core, p), start)
    return pair, block - start


def widest(s, top):
    for i in range(4):
        top = jnp.maximum(top, s[:, i * 128 : (i + 1) * 128])
    return top


def teacher_scores(core, qbuf, kbuf, scores, peak, between):
    scale = math.log2(math.e) / math.sqrt(128.0)
    row = lax.broadcasted_iota(jnp.int32, (512, 512), 0)
    col = lax.broadcasted_iota(jnp.int32, (512, 512), 1)
    for pair in range(4):
        last = chunk_of(core, 2 * pair) // 2
        q = qbuf[pl.ds(pair * 512, 512), :]
        s = jnp.where(col <= row, nt(q, kbuf[rows(last * 512, 512), :]) * scale, -1e30)
        scores[blocks_before(core, pair) + last] = s
        peak[pair] = widest(s, jnp.full((512, 128), -1e30, F32))

    def off_diagonal(step):
        for i in range(SCORE_UNROLL):
            n = step * SCORE_UNROLL + i
            pair = sum(
                (n >= blocks_before(core, p) - p).astype(jnp.int32) for p in range(1, 4)
            )
            block = n + pair
            _, jj = pair_and_key(core, block)
            s = nt(qbuf[rows(pair * 512, 512), :], kbuf[rows(jj * 512, 512), :]) * scale
            scores[block] = s
            peak[pair] = widest(s, peak[pair])

    between(0)
    pl.loop(0, 1)(off_diagonal)
    between(1)
    pl.loop(1, 2)(off_diagonal)
    between(2)
    for pair in range(4):
        peak[pair] = jnp.broadcast_to(jnp.max(peak[pair], axis=1, keepdims=True), (512, 128))


def teacher_weights(core, vext, scores, peak, acc, teacher_out, energy):
    acc[...] = jnp.zeros_like(acc)

    @pl.loop(0, 18 // WEIGHT_UNROLL)
    def _(step):
        for i in range(WEIGHT_UNROLL):
            block = step * WEIGHT_UNROLL + i
            pair, jj = pair_and_key(core, block)
            top = peak[pair]
            total = None
            for h in range(2):
                w = [
                    jnp.exp2(scores[block, :, (2 * h + g) * 128 : (2 * h + g + 1) * 128] - top)
                    for g in range(2)
                ]
                w = jnp.concatenate(w, axis=1).astype(BF16)
                part = nn(w, vext[rows(jj * 512 + h * 256, 256), :])
                total = part if total is None else total + part
            acc[pair] += total

    for pair in range(4):
        t = acc[pair, :, 0:128] / acc[pair, :, 128:256]
        teacher_out[2 * pair] = t[0:256]
        teacher_out[2 * pair + 1] = t[256:512]
        energy[...] += jnp.sum((t * t).reshape(64, 8, 128), axis=0)


SCORE_UNROLL = 7
VALUE_STEPS = ((), (0, 1, 2), ())
WEIGHT_UNROLL = 3


def student(
    core, qbuf, vext, wq_t, teacher_out, phi_hi, phi_lo, state_hi, state_lo, diag, back, mq
):
    wq2 = signed(wq_t)
    mq[...] = jnp.zeros_like(mq)
    row = lax.broadcasted_iota(jnp.int32, (256, 256), 0)
    col = lax.broadcasted_iota(jnp.int32, (256, 256), 1)
    visible = col <= row

    def one(slot):
        chunk = chunk_of(core, slot)
        q = qbuf[rows(slot * 256, 256), :]
        values = vext[rows(chunk * 256, 256), :]
        q2 = jnp.concatenate([q, q], axis=1)
        phi, _ = feature_parts(nt(q2, wq2))
        phi_t, slope_t = feature_parts(nt(wq2, q2))
        qh, ql = split(phi)
        qth, qtl = split(phi_t)
        qhh = jnp.concatenate([qh, qh], axis=1)
        qts = jnp.concatenate([qth, qtl], axis=0)
        kh, kl = phi_hi[chunk], phi_lo[chunk]
        sh, sl = state_hi[chunk], state_lo[chunk]
        ks = jnp.concatenate([kh, kl], axis=0)
        ss = jnp.concatenate([sh, sl], axis=0)
        inner = jnp.where(visible, nn(qhh, ks) + nn(ql, kh), 0.0)
        ih, il = split(inner)
        both = (nn(ih, values) + nn(il, values)) + (nn(qhh, ss) + nn(ql, sh))
        inverse = 1.0 / both[:, 128:256]
        student = both[:, 0:128] * inverse
        grad_out = LOSS_SCALE * (student - teacher_out[slot])
        grad_numer = grad_out * inverse
        gh, gl = split(jnp.concatenate([grad_numer, -(grad_numer * student)], axis=1))
        grad_inner = jnp.where(visible, nt(gh, values) + nt(gl, values), 0.0)
        gih, gil = split(grad_inner)
        back_both = nn(qts, gh)
        back[chunk] = (back_both[0:128] + back_both[128:256]) + nn(qth, gl)
        diag_both = nn(qts, gih)
        diag[chunk] = (diag_both[0:128] + diag_both[128:256]) + nn(qth, gil)
        grad_both = nt(ks, gih) + nt(ss, gh)
        grad_phi = (grad_both[0:128] + grad_both[128:256]) + (nt(kh, gil) + nt(sh, gl))
        dh, dl = split(grad_phi * slope_t)
        m_both = nn(jnp.concatenate([dh, dl], axis=0), q)
        return m_both[0:128] + m_both[128:256]

    @pl.loop(0, 8 // STUDENT_UNROLL)
    def _(step):
        parts = [one(step * STUDENT_UNROLL + h) for h in range(STUDENT_UNROLL)]
        mq[...] += sum(parts[1:], parts[0])


STUDENT_UNROLL = 4


def key_backward(group, kbuf, vext, slope, carry, diag, back, mk):
    later = carry[...]
    total = mk[...]
    for i in range(4):
        j = 15 - (group * 4 + i)
        keys = kbuf[rows(j * 256, 256), :]
        values = vext[rows(j * 256, 256), :]
        lh, ll = split(later)
        g_both = nt(jnp.concatenate([lh, ll], axis=0), values)
        grad_phi = (g_both[0:128] + g_both[128:256]) + diag[j]
        dh, dl = split(grad_phi * slope[j])
        m_both = nn(jnp.concatenate([dh, dl], axis=0), keys)
        total = total + (m_both[0:128] + m_both[128:256])
        later = later + back[j]
    mk[...] = total
    carry[...] = later


def scratch():
    v = pltpu.VMEM
    return [
        v((2048, 128), BF16), v((2048, 128), F32), v((16, 128, 128), BF16),
        v((2048, 128), BF16), v((4096, 128), BF16), v((4096, 128), BF16), v((4096, 256), BF16),
        v((4096, 128), BF16),
        v((64, 128), F32), v((64, 128), F32), v((18, 512, 512), F32), v((4, 512, 256), F32),
        v((4, 512, 128), F32), v((8, 256, 128), F32),
        v((16, 128, 256), BF16), v((16, 128, 256), BF16), v((16, 128, 256), F32),
        v((16, 128, 256), BF16), v((16, 128, 256), BF16), v((128, 256), F32),
        v((16, 128, 256), F32), v((16, 128, 256), F32), v((128, 128), F32), v((128, 128), F32),
        v((8, 128), F32),
    ]


def exchange_scratch():
    v, dma = pltpu.VMEM, pltpu.SemaphoreType.DMA
    return [
        v((32, 128), F32), v((32, 128), F32), v((32, 128), F32), v((32, 128), F32),
        v((8, 8, 128), F32), v((32 * 40, 128), F32), v((32 * 32, 128), F32),
        dma((16,)), dma((16,)), dma((6,)),
    ] + [dma((6,)), dma((6,)), dma((4,)), dma((4,))] * 4 + [dma((2,)), dma((2,)), dma((8,)), dma((8,))]


def on_device(queries, key_states, value_vector_states, map_query, map_key):
    far = pl.BlockSpec(memory_space=pltpu.HBM)
    whole = pl.BlockSpec(memory_space=pltpu.VMEM)
    grad_query, grad_key = pl.pallas_call(
        kernel,
        out_shape=(jax.ShapeDtypeStruct((16, 64, 128), F32),) * 2,
        in_specs=[far] * 5,
        out_specs=(whole, whole),
        scratch_shapes=scratch() + exchange_scratch(),
        compiler_params=pltpu.CompilerParams(
            collective_id=0, has_side_effects=True, vmem_limit_bytes=50 * 1024 * 1024
        ),
        name="transfer_step",
    )(
        *(
            pltpu.with_memory_space_constraint(operand, pltpu.HBM)
            for operand in (
                queries.reshape(2048, 128),
                key_states.reshape(128, 128),
                value_vector_states.reshape(128, 128),
                jnp.swapaxes(map_query, 1, 2),
                jnp.swapaxes(map_key, 1, 2),
            )
        ),
    )
    return jnp.swapaxes(grad_query, 1, 2), jnp.swapaxes(grad_key, 1, 2)


def solution(mesh):
    torus = Mesh(mesh.devices.reshape(4, 4, 2, mesh.shape["head"]), ("x", "y", "c", "z"))
    ctx = ("x", "y", "c")
    in_specs = (
        P(ctx, "z", None),
        P(ctx, "z", None),
        P(ctx, "z", None),
        P("z", None, None),
        P("z", None, None),
    )
    out_specs = (P("z", None, None), P("z", None, None))
    return jax.shard_map(
        on_device, mesh=torus, in_specs=in_specs, out_specs=out_specs, check_vma=False
    )
```
